32 devices in a mesh: grp: 2 (over y), seq: 4 (over z), mdl: 2 (over x), sub: 2 (over core).
Axes of the slice: x: 2, y: 2, z: 4, core: 2. Of those that a mesh axis runs over, the one named last changes fastest.
Arguments:
- tokens: bfloat16 [1024, 8192], P(('grp', 'seq')), parts along dimension 0, may hold values from -6 to 6
- cotangent: bfloat16 [1024, 8192], P(('grp', 'seq')), parts along dimension 0, may hold values from -6 to 6
- w_in: bfloat16 [112, 7, 128, 128], P(('mdl', 'sub'), None, 'seq'), may hold values from -0.1875 to 0.1875
- w_out: bfloat16 [112, 7, 128, 128], P(('mdl', 'sub'), None, 'seq'), may hold values from -0.15625 to 0.15625
- in_blocks: int32 [112, 7], P(('mdl', 'sub')), may hold values from 0 to 63, as said below
- out_blocks: int32 [112, 7], P(('mdl', 'sub')), may hold values from 0 to 63, as said below
Outputs:
- outputs: bfloat16 [1024, 8192], P(('grp', 'seq'), ('mdl', 'sub')), parts along dimension 0
- input_grad: bfloat16 [1024, 8192], P(('grp', 'seq'), ('mdl', 'sub')), parts along dimension 0
The draws below stay inside these ranges and needn't reach their ends.
There are 2 independent parts, one for each index of `grp`. The reference program is written for one: setup_inputs(seed, part) draws one part's arguments, and reference() takes and returns one part's arrays. A program takes and returns all parts, laid end to end along the dimension named above; an argument that names none is the same for every part. Nothing has to cross between parts.
Inputs may be any that keep to these rules, and one draw needn't show every extreme that they name: `in_blocks`: row h lists 7 distinct blocks: a block b(h) and the blocks b(h) xor 2^l for l < 6, all under one relabelling of the blocks of the model width drawn from the seed, with b(h) the block numbered h modulo (64) before relabelling; every block appears. `out_blocks`: built like in_blocks, with a relabelling of its own.
All inputs are finite; a program needn't handle non-finite values.
Results may differ from the reference program's by a relative error of at most 0.009.
Values may be sent and summed in bfloat16 or wider, within the bound.
No kernel may reach another device: no remote copies, remote signals or barrier semaphores. Data moves between devices by JAX's collectives and lax.ppermute only.
A program may use at most 128 MiB of HBM per device.

```python
import jax
import jax.numpy as jnp
from jax import lax

D = 8192
BLK = 128
LEVELS = 6
K = 7
FB = 112
TOKENS = 512
N_MDL = 2
N_SUB = 2


def butterfly_lists(key):
    blocks = D // BLK
    relabel = jax.random.permutation(key, blocks).astype(jnp.int32)
    base = jnp.arange(FB, dtype=jnp.int32) % blocks
    masks = jnp.concatenate([jnp.zeros((1,), jnp.int32), jnp.left_shift(jnp.ones((LEVELS,), jnp.int32), jnp.arange(LEVELS, dtype=jnp.int32))])
    partner = jnp.bitwise_xor(base[:, None], masks[None, :])
    return jnp.take(relabel, partner).astype(jnp.int32)


def draw_in_blocks(key, part):
    return butterfly_lists(jax.random.fold_in(key, 11))


def draw_out_blocks(key, part):
    return butterfly_lists(jax.random.fold_in(key, 23))


def block_levels(key, shape, pieces, least, largest):
    loudness = 1.0
    for axis_at, parts in pieces:
        steps = jax.random.uniform(jax.random.fold_in(jax.random.fold_in(key, 6), axis_at), (parts,), jnp.float32, least / len(pieces), largest / len(pieces))
        loudness = loudness * jnp.repeat(jnp.exp(steps), shape[axis_at] // parts).reshape((-1,) + (1,) * (len(shape) - 1 - axis_at))
    return loudness


def scatter_about(stream_key, shape, width, reach, pieces=(), kind=jnp.bfloat16):
    result = jax.random.normal(stream_key, shape, jnp.float32) * width
    if len(pieces) > 0:
        result = block_levels(stream_key, shape, pieces, -0.22, 0.18) * result
    return jnp.clip(result, min=-reach, max=reach).astype(kind)


def setup_inputs(seed: int = 0, part: int = 0) -> dict:
    keys = jax.random.split(jax.random.key(seed), 7)
    own_keys = jax.random.split(jax.random.fold_in(keys[6], part), 7)
    tokens = scatter_about(own_keys[0], (TOKENS, D), 1.0, 6.0, ((0, 4),))
    cotangent = scatter_about(own_keys[1], (TOKENS, D), 1.0, 6.0, ((0, 4),))
    w_in = scatter_about(keys[2], (FB, K, BLK, BLK), (K * BLK) ** -0.5, 0.1875, ((0, 4), (2, 4)))
    w_out = scatter_about(keys[3], (FB, K, BLK, BLK), (FB * K * BLK // (D // BLK)) ** -0.5, 0.15625, ((0, 4), (2, 4)))
    in_blocks = draw_in_blocks(jax.random.fold_in(keys[6], 71), part)
    out_blocks = draw_out_blocks(jax.random.fold_in(keys[6], 71), part)
    return dict(tokens=tokens, cotangent=cotangent, w_in=w_in, w_out=w_out, in_blocks=in_blocks, out_blocks=out_blocks)


root_half = 0.7071067811865476
inv_root_two_pi = 0.3989422804014327


def gelu_pair(hidden):
    normal_cdf = 0.5 * (1.0 + jax.scipy.special.erf(hidden * root_half))
    density = jnp.exp(-0.5 * hidden * hidden) * inv_root_two_pi
    return hidden * normal_cdf, normal_cdf + hidden * density


def block_sum(block_terms, block_lists, blocks):
    row_count = block_terms.shape[0]
    flattened = block_terms.reshape(row_count, -1, block_terms.shape[-1])
    summed = jnp.zeros((row_count, blocks, block_terms.shape[-1]), jnp.float32)
    summed = summed.at[:, block_lists.reshape(-1), :].add(flattened)
    return summed.reshape(row_count, -1)


def reference(tokens, cotangent, w_in, w_out, in_blocks, out_blocks):
    row_count = tokens.shape[0]
    blocks = D // BLK
    groups = N_MDL * N_SUB
    per_group = FB // groups
    token_blocks = tokens.reshape(row_count, blocks, BLK)
    grad_blocks = cotangent.reshape(row_count, blocks, BLK)

    def one_group(group, carry):
        out_sum, grad_sum = carry
        first = jnp.asarray(group).astype(jnp.int32) * per_group
        weight_in = lax.dynamic_slice_in_dim(w_in, first, per_group, 0).astype(jnp.float32)
        weight_out = lax.dynamic_slice_in_dim(w_out, first, per_group, 0).astype(jnp.float32)
        lists_in = lax.dynamic_slice_in_dim(in_blocks, first, per_group, 0).astype(jnp.int32)
        lists_out = lax.dynamic_slice_in_dim(out_blocks, first, per_group, 0).astype(jnp.int32)
        gathered = jnp.take(token_blocks, lists_in, axis=1).astype(jnp.float32)
        hidden = jnp.einsum("rhki,hkji->rhj", gathered, weight_in)
        activated, slopes = gelu_pair(hidden)
        act_rounded = activated.astype(jnp.bfloat16).astype(jnp.float32)
        out_terms = jnp.einsum("rhi,hkji->rhkj", act_rounded, weight_out)
        part_out = lax.optimization_barrier(block_sum(out_terms, lists_out, blocks).astype(jnp.bfloat16))
        grad_gathered = jnp.take(grad_blocks, lists_out, axis=1).astype(jnp.float32)
        back_act = jnp.einsum("rhkj,hkji->rhi", grad_gathered, weight_out)
        back_hidden = (back_act * slopes).astype(jnp.bfloat16).astype(jnp.float32)
        back_terms = jnp.einsum("rhj,hkji->rhki", back_hidden, weight_in)
        part_in = lax.optimization_barrier(block_sum(back_terms, lists_in, blocks).astype(jnp.bfloat16))
        return (out_sum + part_out.astype(jnp.float32), grad_sum + part_in.astype(jnp.float32))

    start = (jnp.zeros((row_count, D), jnp.float32), jnp.zeros((row_count, D), jnp.float32))
    out_sum, grad_sum = lax.fori_loop(0, groups, one_group, start)
    return (out_sum.astype(jnp.bfloat16), grad_sum.astype(jnp.bfloat16))
```

```python
import functools

import jax
import jax.numpy as jnp
from jax import lax
from jax.experimental import pallas as pl
from jax.experimental.pallas import tpu as pltpu
from jax.sharding import PartitionSpec as P

root_half = 0.7071067811865476
inv_root_two_pi = 0.3989422804014327
F32, BF16 = jnp.float32, jnp.bfloat16
SWAP = [(0, 1), (1, 0)]
VMEM_LIMIT = 60 * 1024 * 1024


def gelu_pair(hidden):
    normal_cdf = 0.5 * (1.0 + lax.erf(hidden * root_half))
    density = jnp.exp(-0.5 * hidden * hidden) * inv_root_two_pi
    return (hidden * normal_cdf, normal_cdf + hidden * density)


def selector(block_lists, blocks):
    flat_lists = block_lists.reshape(-1)
    return (flat_lists[:, None] == jnp.arange(blocks, dtype=jnp.int32)[None, :]).astype(F32)


def flat_terms(block_terms):
    return block_terms.reshape(block_terms.shape[0], -1, block_terms.shape[-1])


def general(tokens, cotangent, w_in, w_out, in_blocks, out_blocks):
    row_count = tokens.shape[0]
    block_size = w_in.shape[3]
    blocks = tokens.shape[1] // block_size
    token_blocks = jnp.take(tokens.reshape(row_count, blocks, block_size), in_blocks, axis=1)
    grad_blocks = jnp.take(cotangent.reshape(row_count, blocks, block_size), out_blocks, axis=1)
    pick_out = selector(out_blocks, blocks)
    pick_in = selector(in_blocks, blocks)
    full_in = lax.all_gather(w_in, "seq", axis=2, tiled=True)
    full_out = lax.all_gather(w_out, "seq", axis=2, tiled=True)
    hidden = jnp.einsum("rhki,hkji->rhj", token_blocks, full_in, preferred_element_type=F32)
    activated, slopes = gelu_pair(hidden)
    out_terms = jnp.einsum(
        "rhi,hkji->rhkj", activated.astype(BF16), full_out, preferred_element_type=F32
    )
    partial_out = jnp.einsum(
        "rsj,sc->rcj", flat_terms(out_terms), pick_out, precision=lax.Precision.HIGHEST
    ).reshape(row_count, -1)
    outputs = lax.psum_scatter(
        partial_out.astype(BF16), ("mdl", "sub"), scatter_dimension=1, tiled=True
    )
    back_act = jnp.einsum("rhkj,hkji->rhi", grad_blocks, full_out, preferred_element_type=F32)
    back_hidden = (back_act * slopes).astype(BF16)
    back_terms = jnp.einsum("rhj,hkji->rhki", back_hidden, full_in, preferred_element_type=F32)
    partial_in = jnp.einsum(
        "rsj,sc->rcj", flat_terms(back_terms), pick_in, precision=lax.Precision.HIGHEST
    ).reshape(row_count, -1)
    input_grad = lax.psum_scatter(
        partial_in.astype(BF16), ("mdl", "sub"), scatter_dimension=1, tiled=True
    )
    return (outputs, input_grad)


def weight_copies(meta, own, ups, downs, dest, sems, group, per_group):
    places = len(ups) + 1
    rows = own.shape[2]
    z = meta[0]
    span = pl.ds(group * per_group, per_group)

    def copy(source, distance):
        place = lax.rem(z - distance + places, places)
        at = pl.ds(pl.multiple_of(place * rows, rows), rows)
        return pltpu.make_async_copy(
            source.at[span], dest.at[span, :, at, :], sems.at[distance, group]
        )

    return copy


def start_weights(meta, own, ups, downs, dest, sems, groups, per_group):
    places = len(ups) + 1
    z = meta[0]

    def body(group, _):
        copy = weight_copies(meta, own, ups, downs, dest, sems, group, per_group)
        copy(own, 0).start()
        for distance in range(1, places):

            @pl.when(z >= distance)
            def _():
                copy(ups[distance - 1], distance).start()

            @pl.when(z < distance)
            def _():
                copy(downs[places - distance - 1], distance).start()

        return 0

    lax.fori_loop(0, groups, body, 0)


def wait_weights(meta, own, ups, downs, dest, sems, group, per_group):
    copy = weight_copies(meta, own, ups, downs, dest, sems, group, per_group)
    for distance in range(len(ups) + 1):
        copy(own, distance).wait()


def row_copies(meta, own, far_a, far_b, dest, sems):
    rows, half = far_a.shape
    s = meta[2]
    first = pl.ds(pl.multiple_of(s * half, half), half)
    second = pl.ds(pl.multiple_of((1 - s) * half, half), half)
    return (
        pltpu.make_async_copy(own, dest.at[pl.ds(0, rows)], sems.at[0]),
        pltpu.make_async_copy(far_a, dest.at[pl.ds(rows, rows), first], sems.at[1]),
        pltpu.make_async_copy(far_b, dest.at[pl.ds(rows, rows), second], sems.at[2]),
    )


def columns(block, size):
    return pl.ds(pl.multiple_of(block * size, size), size)


def gathered(rows_ref, lists, h, slots, size):
    return jnp.concatenate(
        [rows_ref[:, columns(lists[h * slots + k], size)] for k in range(slots)], axis=1
    )


def lanes(weights, slots):
    return jnp.concatenate([weights[k] for k in range(slots)], axis=1)


NT = (((1,), (1,)), ((), ()))
NN = (((1,), (0,)), ((), ()))


def dot(a, b, dims):
    return lax.dot_general(a, b, dims, preferred_element_type=F32)


def hidden_kernel(per_group, places, meta, lists, *refs):
    own, ups, downs = refs[0], refs[1:places], refs[places : 2 * places - 1]
    rows = refs[2 * places - 1 : 2 * places + 2]
    act, slopes, x, w, wsem, xsem = refs[2 * places + 2 :]
    hidden_blocks, slots, size, _ = w.shape
    groups = hidden_blocks // per_group
    copies = row_copies(meta, *rows, x, xsem)
    for c in copies:
        c.start()
    start_weights(meta, own, ups, downs, w, wsem, groups, per_group)
    for c in copies:
        c.wait()

    def body(group, _):
        wait_weights(meta, own, ups, downs, w, wsem, group, per_group)
        for i in range(per_group):
            h = group * per_group + i
            hidden = dot(gathered(x, lists, h, slots, size), lanes(w[h], slots), NT)
            activated, slope = gelu_pair(hidden)
            act[h] = activated.astype(BF16)
            slopes[h] = slope
        return 0

    lax.fori_loop(0, groups, body, 0)


def split_store(meta, total, keep, send):
    width = keep.shape[2]
    m, s = meta[1], meta[2]
    for far in range(2):
        base = 2 * (m if far == 0 else 1 - m)
        keep[far] = total[:, columns(base + s, width)].astype(BF16)
        send[far] = total[:, columns(base + 1 - s, width)].astype(BF16)


def output_kernel(per_group, places, meta, lists, *refs):
    own, ups, downs = refs[0], refs[1:places], refs[places : 2 * places - 1]
    rows = refs[2 * places - 1 : 2 * places + 2]
    act, slopes, keep, send, back, x, w, total, wsem, xsem = refs[2 * places + 2 :]
    hidden_blocks, slots, size, _ = w.shape
    groups = hidden_blocks // per_group
    copies = row_copies(meta, *rows, x, xsem)
    for c in copies:
        c.start()
    start_weights(meta, own, ups, downs, w, wsem, groups, per_group)
    total[...] = jnp.zeros_like(total)
    for c in copies:
        c.wait()

    def body(group, _):
        wait_weights(meta, own, ups, downs, w, wsem, group, per_group)
        for i in range(per_group):
            h = group * per_group + i
            flat = w[h].reshape(slots * size, size)
            back_act = dot(gathered(x, lists, h, slots, size), flat, NN)
            back[h] = (back_act * slopes[h]).astype(BF16)
            terms = dot(act[h], flat, NT)
            for k in range(slots):
                at = columns(lists[h * slots + k], size)
                total[:, at] += terms[:, k * size : (k + 1) * size]
        return 0

    lax.fori_loop(0, groups, body, 0)
    split_store(meta, total, keep, send)


def grad_kernel(per_group, places, meta, lists, *refs):
    own, ups, downs = refs[0], refs[1:places], refs[places : 2 * places - 1]
    back, keep, send, w, total, wsem = refs[2 * places - 1 :]
    hidden_blocks, slots, size, _ = w.shape
    groups = hidden_blocks // per_group
    start_weights(meta, own, ups, downs, w, wsem, groups, per_group)
    total[...] = jnp.zeros_like(total)

    def body(group, _):
        wait_weights(meta, own, ups, downs, w, wsem, group, per_group)
        for i in range(per_group):
            h = group * per_group + i
            terms = dot(back[h], lanes(w[h], slots), NN)
            for k in range(slots):
                at = columns(lists[h * slots + k], size)
                total[:, at] += terms[:, k * size : (k + 1) * size]
        return 0

    lax.fori_loop(0, groups, body, 0)
    split_store(meta, total, keep, send)


def shape(dims, dtype=BF16):
    return jax.ShapeDtypeStruct(dims, dtype)


def call(kernel, name, ins, out_shape, scratch, flops, bytes_accessed):
    spec = {"s": pltpu.SMEM, "h": pl.ANY, "v": pltpu.VMEM}
    args = [a for _, a in ins]
    return pl.pallas_call(
        kernel,
        name=name,
        out_shape=out_shape,
        in_specs=[pl.BlockSpec(memory_space=spec[where]) for where, _ in ins],
        out_specs=jax.tree.map(lambda _: pl.BlockSpec(memory_space=pltpu.VMEM), out_shape),
        scratch_shapes=scratch,
        compiler_params=pltpu.CompilerParams(vmem_limit_bytes=VMEM_LIMIT),
        cost_estimate=pl.CostEstimate(
            flops=flops, bytes_accessed=bytes_accessed, transcendentals=0
        ),
    )(*args)


def ring(own, places):
    ups, downs = [], []
    up = down = own
    for step in range(1, places):
        up = lax.ppermute(up, "seq", [(z, z + 1) for z in range(step - 1, places - 1)])
        down = lax.ppermute(down, "seq", [(z + 1, z) for z in range(0, places - step)])
        ups.append(up)
        downs.append(down)
    return ups, downs


def add(a, b):
    return (a.astype(F32) + b.astype(F32)).astype(BF16)


def reduce_pair(keep, send):
    rows, width = keep.shape[1] // 2, keep.shape[2] // 2
    u = add(keep, lax.ppermute(send, "sub", SWAP))
    x_in = lax.ppermute(u[1, :, :width], "mdl", SWAP)
    y_in = lax.ppermute(u[:, rows:, width:], "grp", SWAP)
    left = add(u[0, :, :width], x_in)
    right = add(u[:, :rows, width:], y_in)
    left_in = lax.ppermute(left[rows:], "grp", SWAP)
    right_in = lax.ppermute(right[1], "mdl", SWAP)
    return jnp.concatenate([add(left[:rows], left_in), add(right[0], right_in)], axis=1)


def fast(tokens, cotangent, w_in, w_out, in_blocks, out_blocks):
    places = lax.axis_size("seq")
    rows, model_width = tokens.shape
    hidden_blocks, slots, _, size = w_in.shape
    mine = hidden_blocks // 2
    grp, z, m, s = (lax.axis_index(a) for a in ("grp", "seq", "mdl", "sub"))
    meta = jnp.stack([z, m, s]).astype(jnp.int32)

    def own_half(a):
        return lax.dynamic_slice_in_dim(a, grp * mine, mine, 0)

    in_list = own_half(in_blocks).reshape(-1)
    out_list = own_half(out_blocks).reshape(-1)
    in_own, out_own = own_half(w_in), own_half(w_out)
    half = model_width // 2

    def far_rows(a):
        piece = lax.ppermute(lax.dynamic_slice_in_dim(a, s * half, half, 1), "grp", SWAP)
        return piece, lax.ppermute(piece, "sub", SWAP)

    in_ups, in_downs = ring(in_own, places)
    tok_a, tok_b = far_rows(tokens)
    cot_a, cot_b = far_rows(cotangent)
    out_ups, out_downs = ring(out_own, places)

    per_group = 2 if mine % 2 == 0 else 1
    groups = mine // per_group
    both = 2 * rows
    w_scratch = pltpu.VMEM((mine, slots, size, size), BF16)
    w_sems = pltpu.SemaphoreType.DMA((places, groups))
    x_scratch = pltpu.VMEM((both, model_width), BF16)
    x_sems = pltpu.SemaphoreType.DMA((3,))
    total = pltpu.VMEM((both, model_width), F32)
    flops = 2 * both * mine * slots * size * size
    out_part = shape((2, both, model_width // 4))

    act, slopes = call(
        functools.partial(hidden_kernel, per_group, places),
        "hidden",
        [("s", meta), ("s", in_list)]
        + [("h", a) for a in [in_own, *in_ups, *in_downs, tokens, tok_a, tok_b]],
        [shape((mine, both, size)), shape((mine, both, size), F32)],
        [x_scratch, w_scratch, w_sems, x_sems],
        flops,
        16 * 2**20,
    )
    keep, send, back = call(
        functools.partial(output_kernel, per_group, places),
        "out_terms",
        [("s", meta), ("s", out_list)]
        + [("h", a) for a in [out_own, *out_ups, *out_downs, cotangent, cot_a, cot_b]]
        + [("v", act), ("v", slopes)],
        [out_part, out_part, shape((mine, both, size))],
        [x_scratch, w_scratch, total, w_sems, x_sems],
        2 * flops,
        16 * 2**20,
    )
    grad_keep, grad_send = call(
        functools.partial(grad_kernel, per_group, places),
        "grad_terms",
        [("s", meta), ("s", in_list)]
        + [("h", a) for a in [in_own, *in_ups, *in_downs]]
        + [("v", back)],
        [out_part, out_part],
        [w_scratch, total, w_sems],
        flops,
        16 * 2**20,
    )
    return reduce_pair(keep, send), reduce_pair(grad_keep, grad_send)


def solution(mesh):
    in_specs = (
        P(("grp", "seq"), None),
        P(("grp", "seq"), None),
        P(("mdl", "sub"), None, "seq", None),
        P(("mdl", "sub"), None, "seq", None),
        P(("mdl", "sub"), None),
        P(("mdl", "sub"), None),
    )
    out_specs = (P(("grp", "seq"), ("mdl", "sub")), P(("grp", "seq"), ("mdl", "sub")))
    sizes = tuple(mesh.shape[a] for a in ("grp", "seq", "mdl", "sub"))
    local = fast if sizes == (2, 4, 2, 2) else general
    return jax.shard_map(local, mesh=mesh, in_specs=in_specs, out_specs=out_specs, check_vma=False)
```

```python
import functools

import jax
import jax.numpy as jnp
from jax import lax
from jax.experimental import pallas as pl
from jax.experimental.pallas import tpu as pltpu
from jax.sharding import PartitionSpec as P

root_half = 0.7071067811865476
inv_root_two_pi = 0.3989422804014327
F32, BF16 = jnp.float32, jnp.bfloat16
SWAP = [(0, 1), (1, 0)]


def gelu_pair(hidden):
    normal_cdf = 0.5 * (1.0 + lax.erf(hidden * root_half))
    density = jnp.exp(-0.5 * hidden * hidden) * inv_root_two_pi
    return (hidden * normal_cdf, normal_cdf + hidden * density)


def selector(block_lists, blocks):
    flat_lists = block_lists.reshape(-1)
    return (flat_lists[:, None] == jnp.arange(blocks, dtype=jnp.int32)[None, :]).astype(F32)


def flat_terms(block_terms):
    return block_terms.reshape(block_terms.shape[0], -1, block_terms.shape[-1])


def general(tokens, cotangent, w_in, w_out, in_blocks, out_blocks):
    row_count = tokens.shape[0]
    block_size = w_in.shape[3]
    blocks = tokens.shape[1] // block_size
    token_blocks = jnp.take(tokens.reshape(row_count, blocks, block_size), in_blocks, axis=1)
    grad_blocks = jnp.take(cotangent.reshape(row_count, blocks, block_size), out_blocks, axis=1)
    pick_out = selector(out_blocks, blocks)
    pick_in = selector(in_blocks, blocks)
    full_in = lax.all_gather(w_in, "seq", axis=2, tiled=True)
    full_out = lax.all_gather(w_out, "seq", axis=2, tiled=True)
    hidden = jnp.einsum("rhki,hkji->rhj", token_blocks, full_in, preferred_element_type=F32)
    activated, slopes = gelu_pair(hidden)
    out_terms = jnp.einsum(
        "rhi,hkji->rhkj", activated.astype(BF16), full_out, preferred_element_type=F32
    )
    partial_out = jnp.einsum(
        "rsj,sc->rcj", flat_terms(out_terms), pick_out, precision=lax.Precision.HIGHEST
    ).reshape(row_count, -1)
    outputs = lax.psum_scatter(
        partial_out.astype(BF16), ("mdl", "sub"), scatter_dimension=1, tiled=True
    )
    back_act = jnp.einsum("rhkj,hkji->rhi", grad_blocks, full_out, preferred_element_type=F32)
    back_hidden = (back_act * slopes).astype(BF16)
    back_terms = jnp.einsum("rhj,hkji->rhki", back_hidden, full_in, preferred_element_type=F32)
    partial_in = jnp.einsum(
        "rsj,sc->rcj", flat_terms(back_terms), pick_in, precision=lax.Precision.HIGHEST
    ).reshape(row_count, -1)
    input_grad = lax.psum_scatter(
        partial_in.astype(BF16), ("mdl", "sub"), scatter_dimension=1, tiled=True
    )
    return (outputs, input_grad)


def weight_copies(meta, own, ups, downs, dest, sems, group, per_group, first=0):
    places = len(ups) + 1
    rows = own.shape[2]
    z = meta[0]
    span = pl.ds(group * per_group, per_group)
    source_span = pl.ds(first + group * per_group, per_group)

    def copy(source, distance):
        place = lax.rem(z - distance + places, places)
        at = pl.ds(pl.multiple_of(place * rows, rows), rows)
        return pltpu.make_async_copy(
            source.at[source_span], dest.at[span, :, at, :], sems.at[distance, group]
        )

    return copy


def start_weights(meta, own, ups, downs, dest, sems, groups, per_group, first=0):
    places = len(ups) + 1
    z = meta[0]

    def body(group, _):
        copy = weight_copies(meta, own, ups, downs, dest, sems, group, per_group, first)
        copy(own, 0).start()
        for distance in range(1, places):

            @pl.when(z >= distance)
            def _():
                copy(ups[distance - 1], distance).start()

            @pl.when(z < distance)
            def _():
                copy(downs[places - distance - 1], distance).start()

        return 0

    lax.fori_loop(0, groups, body, 0)


def wait_weights(meta, own, ups, downs, dest, sems, group, per_group, first=0):
    copy = weight_copies(meta, own, ups, downs, dest, sems, group, per_group, first)
    for distance in range(len(ups) + 1):
        copy(own, distance).wait()


def row_copies(meta, own, far_a, far_b, dest, sems):
    rows, half = far_a.shape
    s = meta[2]
    first = pl.ds(pl.multiple_of(s * half, half), half)
    second = pl.ds(pl.multiple_of((1 - s) * half, half), half)
    return (
        pltpu.make_async_copy(own, dest.at[pl.ds(0, rows)], sems.at[0]),
        pltpu.make_async_copy(far_a, dest.at[pl.ds(rows, rows), first], sems.at[1]),
        pltpu.make_async_copy(far_b, dest.at[pl.ds(rows, rows), second], sems.at[2]),
    )


def columns(block, size):
    return pl.ds(pl.multiple_of(block * size, size), size)


def gathered(rows_ref, lists, h, slots, size):
    return jnp.concatenate(
        [rows_ref[:, columns(lists[h * slots + k], size)] for k in range(slots)], axis=1
    )


def lanes(weights, slots):
    return jnp.concatenate([weights[k] for k in range(slots)], axis=1)


NT = (((1,), (1,)), ((), ()))
NN = (((1,), (0,)), ((), ()))


def dot(a, b, dims):
    return lax.dot_general(a, b, dims, preferred_element_type=F32)


def hidden_kernel(per_group, places, meta, lists, *refs):
    own, ups, downs = refs[0], refs[1:places], refs[places : 2 * places - 1]
    rows = refs[2 * places - 1 : 2 * places + 2]
    act, slopes, x, w, wsem, xsem = refs[2 * places + 2 :]
    hidden_blocks, slots, size, _ = w.shape
    groups = hidden_blocks // per_group
    copies = row_copies(meta, *rows, x, xsem)
    for c in copies:
        c.start()
    start_weights(meta, own, ups, downs, w, wsem, groups, per_group)
    for c in copies:
        c.wait()

    def body(group, _):
        wait_weights(meta, own, ups, downs, w, wsem, group, per_group)
        for i in range(per_group):
            h = group * per_group + i
            hidden = dot(gathered(x, lists, h, slots, size), lanes(w[h], slots), NT)
            activated, slope = gelu_pair(hidden)
            act[h] = activated.astype(BF16)
            slopes[h] = slope
        return 0

    lax.fori_loop(0, groups, body, 0)


def column_pieces(meta):
    m, s = meta[1], meta[2]
    return [(2 * m + s, 2 * m + 1 - s), (2 * (1 - m) + s, 2 * (1 - m) + 1 - s)]


def split_store(meta, total, keep, send, stage, sems):
    width = keep.shape[2]
    copies = []
    for far, (kept, sent) in enumerate(column_pieces(meta)):
        for i, (at, dest) in enumerate([(sent, send), (kept, keep)]):
            n = 2 * far + i
            stage[n] = total[:, columns(at, width)].astype(BF16)
            copies.append(pltpu.make_async_copy(stage.at[n], dest.at[far], sems.at[n]))
            copies[-1].start()
    for c in copies:
        c.wait()


def add_terms(total, lists, h, terms, slots, size):
    for k in range(slots):
        at = columns(lists[h * slots + k], size)
        total[:, at] += terms[:, k * size : (k + 1) * size]


def early_kernel(per_group, places, first, meta, in_list, out_list, *refs):
    shards = 2 * places - 1
    w_in, w_out = refs[:shards], refs[shards : 2 * shards]
    rows, (act, slopes) = refs[2 * shards : 2 * shards + 3], refs[2 * shards + 3 : 2 * shards + 5]
    out, grad, x, wi, wo, total, total_g, isem, osem, xsem = refs[2 * shards + 5 :]
    hidden_blocks, slots, size, _ = wo.shape
    groups = hidden_blocks // per_group
    into = (meta, w_in[0], w_in[1:places], w_in[places:], wi, isem)
    outof = (meta, w_out[0], w_out[1:places], w_out[places:], wo, osem)
    copies = row_copies(meta, *rows, x, xsem)
    for c in copies:
        c.start()
    start_weights(*outof, groups, per_group)
    start_weights(*into, groups, per_group)
    total[...] = jnp.zeros_like(total)
    total_g[...] = jnp.zeros_like(total_g)
    for c in copies:
        c.wait()

    def body(group, _):
        wait_weights(*outof, group, per_group)
        wait_weights(*into, group, per_group)
        for i in range(per_group):
            h = group * per_group + i
            flat = wo[h].reshape(slots * size, size)
            back_act = dot(gathered(x, out_list, h, slots, size), flat, NN)
            back = (back_act * slopes[h]).astype(BF16)
            add_terms(total, out_list, h, dot(act[h], flat, NT), slots, size)
            add_terms(total_g, in_list, h, dot(back, lanes(wi[h], slots), NN), slots, size)
        return 0

    lax.fori_loop(0, groups, body, 0)
    out[...] = total[...].astype(BF16)
    grad[...] = total_g[...].astype(BF16)


def late_out_kernel(per_group, places, first, meta, lists, *refs):
    shards = 2 * places - 1
    own, ups, downs = refs[0], refs[1:places], refs[places:shards]
    rows, (act, slopes, early) = refs[shards : shards + 3], refs[shards + 3 : shards + 6]
    keep, send, back, x, w, total, stage, wsem, xsem, ssem = refs[shards + 6 :]
    hidden_blocks, slots, size, _ = w.shape
    groups = hidden_blocks // per_group
    copies = row_copies(meta, *rows, x, xsem)
    for c in copies:
        c.start()
    start_weights(meta, own, ups, downs, w, wsem, groups, per_group)
    total[...] = early[...].astype(F32)
    for c in copies:
        c.wait()

    def body(group, _):
        wait_weights(meta, own, ups, downs, w, wsem, group, per_group)
        for i in range(per_group):
            h = group * per_group + i
            flat = w[h].reshape(slots * size, size)
            back_act = dot(gathered(x, lists, first + h, slots, size), flat, NN)
            back[h] = (back_act * slopes[first + h]).astype(BF16)
            add_terms(total, lists, first + h, dot(act[first + h], flat, NT), slots, size)
        return 0

    lax.fori_loop(0, groups, body, 0)
    split_store(meta, total, keep, send, stage, ssem)


def late_grad_kernel(per_group, places, first, meta, lists, *refs):
    shards = 2 * places - 1
    own, ups, downs = refs[0], refs[1:places], refs[places:shards]
    back, early, keep, send, w, total, stage, wsem, ssem = refs[shards:]
    hidden_blocks, slots, size, _ = w.shape
    groups = hidden_blocks // per_group
    start_weights(meta, own, ups, downs, w, wsem, groups, per_group, first)
    total[...] = early[...].astype(F32)

    def body(group, _):
        wait_weights(meta, own, ups, downs, w, wsem, group, per_group, first)
        for i in range(per_group):
            h = group * per_group + i
            add_terms(total, lists, first + h, dot(back[h], lanes(w[h], slots), NN), slots, size)
        return 0

    lax.fori_loop(0, groups, body, 0)
    split_store(meta, total, keep, send, stage, ssem)


def shape(dims, dtype=BF16):
    return jax.ShapeDtypeStruct(dims, dtype)


def call(kernel, name, ins, outs, scratch, vmem_mib, flops, bytes_accessed):
    spec = {"s": pltpu.SMEM, "h": pl.ANY, "v": pltpu.VMEM}
    args = [a for _, a in ins]
    out_shape = [a for _, a in outs]
    return pl.pallas_call(
        kernel,
        name=name,
        out_shape=out_shape,
        in_specs=[pl.BlockSpec(memory_space=spec[where]) for where, _ in ins],
        out_specs=[pl.BlockSpec(memory_space=spec[where]) for where, _ in outs],
        scratch_shapes=scratch,
        compiler_params=pltpu.CompilerParams(vmem_limit_bytes=vmem_mib * 2**20),
        cost_estimate=pl.CostEstimate(
            flops=flops, bytes_accessed=bytes_accessed, transcendentals=0
        ),
    )(*args)


def after(value, *others):
    return lax.optimization_barrier((value, *others))[0]


def hop(up, down, step, places):
    return (
        lax.ppermute(up, "seq", [(z, z + 1) for z in range(step - 1, places - 1)]),
        lax.ppermute(down, "seq", [(z + 1, z) for z in range(0, places - step)]),
    )


def rings(pieces, order, waits, places):
    state = {i: (p, p) for i, p in enumerate(pieces)}
    arrived = {i: ([], []) for i in range(len(pieces))}
    hops = []
    for n, (i, step) in enumerate(order):
        up, down = state[i]
        if n in waits:
            up, down = after(up, hops[waits[n]][0]), after(down, hops[waits[n]][1])
        up, down = hop(up, down, step, places)
        state[i] = (up, down)
        hops.append((up, down))
        arrived[i][0].append(up)
        arrived[i][1].append(down)
    return [arrived[i] for i in range(len(pieces))], hops


def add(a, b):
    return (a.astype(F32) + b.astype(F32)).astype(BF16)


def reduce_pair(keep, send):
    rows, width = keep.shape[1] // 2, keep.shape[2] // 2
    u = add(keep, lax.ppermute(send, "sub", SWAP))
    x_in = lax.ppermute(u[1, :, :width], "mdl", SWAP)
    y_in = lax.ppermute(u[:, rows:, width:], "grp", SWAP)
    left = add(u[0, :, :width], x_in)
    right = add(u[:, :rows, width:], y_in)
    left_in = lax.ppermute(left[rows:], "grp", SWAP)
    right_in = lax.ppermute(right[1], "mdl", SWAP)
    return jnp.concatenate([add(left[:rows], left_in), add(right[0], right_in)], axis=1)


def fast(tokens, cotangent, w_in, w_out, in_blocks, out_blocks):
    places = lax.axis_size("seq")
    rows, model_width = tokens.shape
    hidden_blocks, slots, shard_rows, size = w_in.shape
    mine = hidden_blocks // 2
    late = 6
    early = mine - late
    grp, z, m, s = (lax.axis_index(a) for a in ("grp", "seq", "mdl", "sub"))
    meta = jnp.stack([z, m, s]).astype(jnp.int32)

    def own_part(a, first, count):
        start = (grp * mine + first,) + (0,) * (a.ndim - 1)
        return lax.dynamic_slice(a, start, (count,) + a.shape[1:])

    in_list = own_part(in_blocks, 0, mine).reshape(-1)
    out_list = own_part(out_blocks, 0, mine).reshape(-1)
    half = model_width // 2

    pieces = [own_part(w_in, 0, mine), own_part(w_out, 0, early), own_part(w_out, early, late)]
    order = [(0, 1), (1, 1), (0, 2), (1, 2), (0, 3), (2, 1), (1, 3), (2, 2), (2, 3)]
    shards, hops = rings(pieces, order, {5: 2, 6: 3}, places)
    (in_w, early_w, late_w) = [(p, *u, *d) for p, (u, d) in zip(pieces, shards)]

    def far_rows(a, *behind):
        piece = lax.ppermute(lax.dynamic_slice_in_dim(a, s * half, half, 1), "grp", SWAP)
        return piece, lax.ppermute(after(piece, *behind), "sub", SWAP)

    tok = far_rows(tokens, *hops[2])
    cot = far_rows(cotangent, *hops[4])

    per_group = 2
    both = 2 * rows

    def weights(count):
        return pltpu.VMEM((count, slots, size, size), BF16)

    def sems(count):
        return pltpu.SemaphoreType.DMA((places, count // per_group))

    x_scratch = pltpu.VMEM((both, model_width), BF16)
    x_sems = pltpu.SemaphoreType.DMA((3,))
    total = pltpu.VMEM((both, model_width), F32)
    flops = 2 * both * slots * size * size
    quarter = model_width // 4
    out_part = ("h", shape((2, both, quarter)))
    stage = pltpu.VMEM((4, both, quarter), BF16)
    stage_sems = pltpu.SemaphoreType.DMA((4,))

    def hbm(*arrays):
        return [("h", a) for a in arrays]

    act, slopes = call(
        functools.partial(hidden_kernel, per_group, places),
        "hidden",
        [("s", meta), ("s", in_list)] + hbm(*in_w, tokens, *tok),
        [("v", shape((mine, both, size))), ("v", shape((mine, both, size), F32))],
        [x_scratch, weights(mine), sems(mine), x_sems],
        20,
        mine * flops,
        16 * 2**20,
    )
    out_early, grad_early = call(
        functools.partial(early_kernel, per_group, places, 0),
        "early_terms",
        [("s", meta), ("s", in_list), ("s", out_list)]
        + hbm(*in_w, *early_w, cotangent, *cot)
        + [("v", act), ("v", slopes)],
        [("v", shape((both, model_width)))] * 2,
        [x_scratch, weights(early), weights(early), total, total]
        + [sems(early), sems(early), x_sems],
        52,
        3 * early * flops,
        24 * 2**20,
    )
    keep, send, back = call(
        functools.partial(late_out_kernel, per_group, places, early),
        "late_out",
        [("s", meta), ("s", out_list)]
        + hbm(*late_w, cotangent, *cot)
        + [("v", act), ("v", slopes), ("v", out_early)],
        [out_part, out_part, ("v", shape((late, both, size)))],
        [x_scratch, weights(late), total, stage, sems(late), x_sems, stage_sems],
        44,
        2 * late * flops,
        16 * 2**20,
    )
    grad_keep, grad_send = call(
        functools.partial(late_grad_kernel, per_group, places, early),
        "late_grad",
        [("s", meta), ("s", in_list)] + hbm(*in_w) + [("v", back), ("v", grad_early)],
        [out_part, out_part],
        [weights(late), total, stage, sems(late), stage_sems],
        36,
        late * flops,
        16 * 2**20,
    )
    return reduce_pair(keep, send), reduce_pair(grad_keep, grad_send)


def solution(mesh):
    in_specs = (
        P(("grp", "seq"), None),
        P(("grp", "seq"), None),
        P(("mdl", "sub"), None, "seq", None),
        P(("mdl", "sub"), None, "seq", None),
        P(("mdl", "sub"), None),
        P(("mdl", "sub"), None),
    )
    out_specs = (P(("grp", "seq"), ("mdl", "sub")), P(("grp", "seq"), ("mdl", "sub")))
    sizes = tuple(mesh.shape[a] for a in ("grp", "seq", "mdl", "sub"))
    local = fast if sizes == (2, 4, 2, 2) else general
    return jax.shard_map(local, mesh=mesh, in_specs=in_specs, out_specs=out_specs, check_vma=False)
```

```python
import functools

import jax
import jax.numpy as jnp
from jax import lax
from jax.experimental import pallas as pl
from jax.experimental.pallas import tpu as pltpu
from jax.sharding import PartitionSpec as P

root_half = 0.7071067811865476
inv_root_two_pi = 0.3989422804014327
F32, BF16 = jnp.float32, jnp.bfloat16
SWAP = [(0, 1), (1, 0)]


def gelu_pair(hidden):
    normal_cdf = 0.5 * (1.0 + lax.erf(hidden * root_half))
    density = jnp.exp(-0.5 * hidden * hidden) * inv_root_two_pi
    return (hidden * normal_cdf, normal_cdf + hidden * density)


def selector(block_lists, blocks):
    flat_lists = block_lists.reshape(-1)
    return (flat_lists[:, None] == jnp.arange(blocks, dtype=jnp.int32)[None, :]).astype(F32)


def flat_terms(block_terms):
    return block_terms.reshape(block_terms.shape[0], -1, block_terms.shape[-1])


def general(tokens, cotangent, w_in, w_out, in_blocks, out_blocks):
    row_count = tokens.shape[0]
    block_size = w_in.shape[3]
    blocks = tokens.shape[1] // block_size
    token_blocks = jnp.take(tokens.reshape(row_count, blocks, block_size), in_blocks, axis=1)
    grad_blocks = jnp.take(cotangent.reshape(row_count, blocks, block_size), out_blocks, axis=1)
    pick_out = selector(out_blocks, blocks)
    pick_in = selector(in_blocks, blocks)
    full_in = lax.all_gather(w_in, "seq", axis=2, tiled=True)
    full_out = lax.all_gather(w_out, "seq", axis=2, tiled=True)
    hidden = jnp.einsum("rhki,hkji->rhj", token_blocks, full_in, preferred_element_type=F32)
    activated, slopes = gelu_pair(hidden)
    out_terms = jnp.einsum(
        "rhi,hkji->rhkj", activated.astype(BF16), full_out, preferred_element_type=F32
    )
    partial_out = jnp.einsum(
        "rsj,sc->rcj", flat_terms(out_terms), pick_out, precision=lax.Precision.HIGHEST
    ).reshape(row_count, -1)
    outputs = lax.psum_scatter(
        partial_out.astype(BF16), ("mdl", "sub"), scatter_dimension=1, tiled=True
    )
    back_act = jnp.einsum("rhkj,hkji->rhi", grad_blocks, full_out, preferred_element_type=F32)
    back_hidden = (back_act * slopes).astype(BF16)
    back_terms = jnp.einsum("rhj,hkji->rhki", back_hidden, full_in, preferred_element_type=F32)
    partial_in = jnp.einsum(
        "rsj,sc->rcj", flat_terms(back_terms), pick_in, precision=lax.Precision.HIGHEST
    ).reshape(row_count, -1)
    input_grad = lax.psum_scatter(
        partial_in.astype(BF16), ("mdl", "sub"), scatter_dimension=1, tiled=True
    )
    return (outputs, input_grad)


def columns(block, size):
    return pl.ds(pl.multiple_of(block * size, size), size)


class Weights:
    def __init__(self, meta, shards, dest, sems, per_group):
        places = (len(shards) + 1) // 2
        self.own, self.ups, self.downs = shards[0], shards[1:places], shards[places:]
        self.z, self.dest, self.sems = meta[0], dest, sems
        self.places, self.per_group = places, per_group

    def copy(self, source, distance, group):
        rows = source.shape[2]
        place = lax.rem(self.z - distance + self.places, self.places)
        span = pl.ds(group * self.per_group, self.per_group)
        at = pl.ds(pl.multiple_of(place * rows, rows), rows)
        return pltpu.make_async_copy(
            source.at[span], self.dest.at[span, :, at, :], self.sems.at[distance, group]
        )

    def start(self, group):
        self.copy(self.own, 0, group).start()
        for distance in range(1, self.places):

            @pl.when(self.z >= distance)
            def _():
                self.copy(self.ups[distance - 1], distance, group).start()

            @pl.when(self.z < distance)
            def _():
                self.copy(self.downs[self.places - distance - 1], distance, group).start()

    def wait(self, group):
        for distance in range(self.places):
            self.copy(self.own, distance, group).wait()


def row_copies(meta, own, far_a, far_b, dest, sems):
    rows, half = far_a.shape
    s = meta[2]
    first = pl.ds(pl.multiple_of(s * half, half), half)
    second = pl.ds(pl.multiple_of((1 - s) * half, half), half)
    return (
        pltpu.make_async_copy(own, dest.at[pl.ds(0, rows)], sems.at[0]),
        pltpu.make_async_copy(far_a, dest.at[pl.ds(rows, rows), first], sems.at[1]),
        pltpu.make_async_copy(far_b, dest.at[pl.ds(rows, rows), second], sems.at[2]),
    )


NT = (((1,), (1,)), ((), ()))
NN = (((1,), (0,)), ((), ()))


def dot(a, b, dims):
    return lax.dot_general(a, b, dims, preferred_element_type=F32)


def terms_kernel(shards, per_group, first, final, meta, in_list, out_list, *refs):
    refs = list(refs)
    weight_refs = [refs.pop(0) for _ in range(shards)]
    tok, cot = [refs.pop(0) for _ in range(3)], [refs.pop(0) for _ in range(3)]
    before = [refs.pop(0) for _ in range(2)] if final else None
    outs = [refs.pop(0) for _ in range(4 if final else 2)]
    x, c, w, act, slopes, total, total_g, stage, wsem, xsem, csem, bsem, ssem = refs
    count, (_, slots, size, _) = act.shape[0], w.shape
    groups = count // per_group
    weights = Weights(meta, weight_refs, w, wsem, per_group)
    base = meta[3] + first

    tok_copies = row_copies(meta, *tok, x, xsem)
    cot_copies = row_copies(meta, *cot, c, csem)
    for copy in tok_copies:
        copy.start()
    for group in range(groups):
        weights.start(group)
    for copy in cot_copies:
        copy.start()
    for group in range(groups):
        weights.start(groups + group)
    if final:
        early = [pltpu.make_async_copy(before[i], stage.at[i], bsem.at[i]) for i in range(2)]
        for copy in early:
            copy.start()
    total[...] = jnp.zeros_like(total)
    total_g[...] = jnp.zeros_like(total_g)

    def lanes(h):
        return jnp.concatenate([w[h, k] for k in range(slots)], axis=1)

    def gathered(rows_ref, lists, h):
        return jnp.concatenate(
            [rows_ref[:, columns(lists[base + h, k], size)] for k in range(slots)], axis=1
        )

    def add_terms(sums, lists, h, terms):
        for k in range(slots):
            sums[:, columns(lists[base + h, k], size)] += terms[:, k * size : (k + 1) * size]

    for copy in tok_copies:
        copy.wait()

    def forward(group, _):
        weights.wait(group)
        for i in range(per_group):
            h = group * per_group + i
            activated, slope = gelu_pair(dot(gathered(x, in_list, h), lanes(h), NT))
            act[h] = activated.astype(BF16)
            slopes[h] = slope
        return 0

    lax.fori_loop(0, groups, forward, 0)
    for copy in cot_copies:
        copy.wait()

    def backward(group, _):
        weights.wait(groups + group)
        for i in range(per_group):
            h = group * per_group + i
            flat = w[count + h].reshape(slots * size, size)
            back_act = dot(gathered(c, out_list, h), flat, NN)
            back = (back_act * slopes[h]).astype(BF16)
            add_terms(total, out_list, h, dot(act[h], flat, NT))
            add_terms(total_g, in_list, h, dot(back, lanes(h), NN))
        return 0

    lax.fori_loop(0, groups, backward, 0)

    copies = []
    if final:
        for copy in early:
            copy.wait()
        m, s = meta[1], meta[2]
        width = total.shape[1] // 4
        for out, sums in enumerate((total, total_g)):
            keep, send = outs[2 * out], outs[2 * out + 1]
            for far in range(2):
                row = 2 * (m if far == 0 else 1 - m)
                for i, (block, dest) in enumerate([(row + 1 - s, send), (row + s, keep)]):
                    at = columns(block, width)
                    stage[out, :, at] = (sums[:, at] + stage[out, :, at].astype(F32)).astype(BF16)
                    copies.append(
                        pltpu.make_async_copy(
                            stage.at[out, :, at], dest.at[far], ssem.at[4 * out + 2 * far + i]
                        )
                    )
                    copies[-1].start()
    else:
        for out, sums in enumerate((total, total_g)):
            stage[out] = sums[...].astype(BF16)
            copies.append(pltpu.make_async_copy(stage.at[out], outs[out], ssem.at[out]))
            copies[-1].start()
    for copy in copies:
        copy.wait()


def shape(dims, dtype=BF16):
    return jax.ShapeDtypeStruct(dims, dtype)


def terms(name, first, meta, lists, weights, tok, cot, before=()):
    rows, model_width = tok[0].shape
    both, quarter = 2 * rows, model_width // 4
    blocks, slots, _, size = weights[0].shape
    count = blocks // 2
    per_group = 2 if count % 2 == 0 else 1
    places = (len(weights) + 1) // 2
    final = len(before) > 0
    hbm, smem = pl.BlockSpec(memory_space=pltpu.HBM), pl.BlockSpec(memory_space=pltpu.SMEM)
    operands = [*weights, *tok, *cot, *before]
    if final:
        outs = [shape((2, both, quarter))] * 4
    else:
        outs = [shape((both, model_width))] * 2
    return pl.pallas_call(
        functools.partial(terms_kernel, len(weights), per_group, first, final),
        name=name,
        out_shape=outs,
        in_specs=[smem] * 3 + [hbm] * len(operands),
        out_specs=[hbm] * len(outs),
        scratch_shapes=[
            pltpu.VMEM((both, model_width), BF16),
            pltpu.VMEM((both, model_width), BF16),
            pltpu.VMEM((2 * count, slots, size, size), BF16),
            pltpu.VMEM((count, both, size), BF16),
            pltpu.VMEM((count, both, size), F32),
            pltpu.VMEM((both, model_width), F32),
            pltpu.VMEM((both, model_width), F32),
            pltpu.VMEM((2, both, model_width), BF16),
            pltpu.SemaphoreType.DMA((places, 2 * count // per_group)),
            pltpu.SemaphoreType.DMA((3,)),
            pltpu.SemaphoreType.DMA((3,)),
            pltpu.SemaphoreType.DMA((2,)),
            pltpu.SemaphoreType.DMA((8,)),
        ],
        compiler_params=pltpu.CompilerParams(vmem_limit_bytes=52 * 2**20),
        cost_estimate=pl.CostEstimate(
            flops=8 * both * count * slots * size * size,
            bytes_accessed=32 * 2**20,
            transcendentals=2 * count * both * size,
        ),
    )(meta, *lists, *operands)


def tie(values, others):
    return lax.optimization_barrier((tuple(values), tuple(others)))[0]


def hop(pair, name, step, places):
    with jax.named_scope(name):
        return (
            lax.ppermute(pair[0], "seq", [(z, z + 1) for z in range(step - 1, places - 1)]),
            lax.ppermute(pair[1], "seq", [(z + 1, z) for z in range(0, places - step)]),
        )


def add(a, b):
    return (a.astype(F32) + b.astype(F32)).astype(BF16)


def reduce_pair(keep, send):
    rows, width = keep.shape[1] // 2, keep.shape[2] // 2
    u = add(keep, lax.ppermute(send, "sub", SWAP))
    x_in = lax.ppermute(u[1, :, :width], "mdl", SWAP)
    y_in = lax.ppermute(u[:, rows:, width:], "grp", SWAP)
    left = add(u[0, :, :width], x_in)
    right = add(u[:, :rows, width:], y_in)
    left_in = lax.ppermute(left[rows:], "grp", SWAP)
    right_in = lax.ppermute(right[1], "mdl", SWAP)
    return jnp.concatenate([add(left[:rows], left_in), add(right[0], right_in)], axis=1)


def fast(tokens, cotangent, w_in, w_out, in_blocks, out_blocks):
    places = lax.axis_size("seq")
    model_width = tokens.shape[1]
    mine = w_in.shape[0] // 2
    late = 6
    early = mine - late
    grp, z, m, s = (lax.axis_index(a) for a in ("grp", "seq", "mdl", "sub"))
    meta = jnp.stack([z, m, s, grp * mine]).astype(jnp.int32)
    lists = (in_blocks, out_blocks)
    half = model_width // 2

    def part(first, count):
        start = (grp * mine + first, 0, 0, 0)
        size = (count,) + w_in.shape[1:]
        return jnp.concatenate([lax.dynamic_slice(w, start, size) for w in (w_in, w_out)], axis=0)

    p, q = part(0, early), part(early, late)
    tok_half = lax.dynamic_slice_in_dim(tokens, s * half, half, 1)
    cot_half = lax.dynamic_slice_in_dim(cotangent, s * half, half, 1)

    p1 = hop((p, p), "p1", 1, places)
    q1 = hop((q, q), "q1", 1, places)
    tok_a = lax.ppermute(tok_half, "grp", SWAP)
    p2 = hop(tie(p1, ()), "p2", 2, places)
    q2 = hop(tie(q1, ()), "q2", 2, places)
    (cot_half,) = tie((cot_half,), (tok_a,))
    cot_a = lax.ppermute(cot_half, "grp", SWAP)
    p3 = hop(tie(p2, ()), "p3", 3, places)
    q3 = hop(tie(q2, ()), "q3", 3, places)
    tok_b = lax.ppermute(tok_a, "sub", SWAP)
    cot_b = lax.ppermute(cot_a, "sub", SWAP)

    p_all = (p, p1[0], p2[0], p3[0], p1[1], p2[1], p3[1])
    q_all = (q, q1[0], q2[0], q3[0], q1[1], q2[1], q3[1])
    tok, cot = (tokens, tok_a, tok_b), (cotangent, cot_a, cot_b)
    before = terms("early_terms", 0, meta, lists, p_all, tok, cot)
    keep, send, grad_keep, grad_send = terms(
        "late_terms", early, meta, lists, q_all, tok, cot, before
    )
    return reduce_pair(keep, send), reduce_pair(grad_keep, grad_send)


def solution(mesh):
    in_specs = (
        P(("grp", "seq"), None),
        P(("grp", "seq"), None),
        P(("mdl", "sub"), None, "seq", None),
        P(("mdl", "sub"), None, "seq", None),
        P(("mdl", "sub"), None),
        P(("mdl", "sub"), None),
    )
    out_specs = (P(("grp", "seq"), ("mdl", "sub")), P(("grp", "seq"), ("mdl", "sub")))
    sizes = tuple(mesh.shape[a] for a in ("grp", "seq", "mdl", "sub"))
    local = fast if sizes == (2, 4, 2, 2) else general
    return jax.shard_map(local, mesh=mesh, in_specs=in_specs, out_specs=out_specs, check_vma=False)
```

```python
import functools

import jax
import jax.numpy as jnp
from jax import lax
from jax.experimental import pallas as pl
from jax.experimental.pallas import tpu as pltpu
from jax.sharding import PartitionSpec as P

root_half = 0.7071067811865476
inv_root_two_pi = 0.3989422804014327
F32, BF16 = jnp.float32, jnp.bfloat16
SWAP = [(0, 1), (1, 0)]


def gelu_pair(hidden):
    normal_cdf = 0.5 * (1.0 + lax.erf(hidden * root_half))
    density = jnp.exp(-0.5 * hidden * hidden) * inv_root_two_pi
    return (hidden * normal_cdf, normal_cdf + hidden * density)


def selector(block_lists, blocks):
    flat_lists = block_lists.reshape(-1)
    return (flat_lists[:, None] == jnp.arange(blocks, dtype=jnp.int32)[None, :]).astype(F32)


def flat_terms(block_terms):
    return block_terms.reshape(block_terms.shape[0], -1, block_terms.shape[-1])


def general(tokens, cotangent, w_in, w_out, in_blocks, out_blocks):
    row_count = tokens.shape[0]
    block_size = w_in.shape[3]
    blocks = tokens.shape[1] // block_size
    token_blocks = jnp.take(tokens.reshape(row_count, blocks, block_size), in_blocks, axis=1)
    grad_blocks = jnp.take(cotangent.reshape(row_count, blocks, block_size), out_blocks, axis=1)
    pick_out = selector(out_blocks, blocks)
    pick_in = selector(in_blocks, blocks)
    full_in = lax.all_gather(w_in, "seq", axis=2, tiled=True)
    full_out = lax.all_gather(w_out, "seq", axis=2, tiled=True)
    hidden = jnp.einsum("rhki,hkji->rhj", token_blocks, full_in, preferred_element_type=F32)
    activated, slopes = gelu_pair(hidden)
    out_terms = jnp.einsum(
        "rhi,hkji->rhkj", activated.astype(BF16), full_out, preferred_element_type=F32
    )
    partial_out = jnp.einsum(
        "rsj,sc->rcj", flat_terms(out_terms), pick_out, precision=lax.Precision.HIGHEST
    ).reshape(row_count, -1)
    outputs = lax.psum_scatter(
        partial_out.astype(BF16), ("mdl", "sub"), scatter_dimension=1, tiled=True
    )
    back_act = jnp.einsum("rhkj,hkji->rhi", grad_blocks, full_out, preferred_element_type=F32)
    back_hidden = (back_act * slopes).astype(BF16)
    back_terms = jnp.einsum("rhj,hkji->rhki", back_hidden, full_in, preferred_element_type=F32)
    partial_in = jnp.einsum(
        "rsj,sc->rcj", flat_terms(back_terms), pick_in, precision=lax.Precision.HIGHEST
    ).reshape(row_count, -1)
    input_grad = lax.psum_scatter(
        partial_in.astype(BF16), ("mdl", "sub"), scatter_dimension=1, tiled=True
    )
    return (outputs, input_grad)


def columns(block, size):
    return pl.ds(pl.multiple_of(block * size, size), size)


class Weights:
    def __init__(self, meta, shards, dest, sems, per_group):
        places = (len(shards) + 1) // 2
        self.own, self.ups, self.downs = shards[0], shards[1:places], shards[places:]
        self.z, self.dest, self.sems = meta[0], dest, sems
        self.places, self.per_group = places, per_group

    def copy(self, source, distance, group):
        rows = source.shape[2]
        place = lax.rem(self.z - distance + self.places, self.places)
        span = pl.ds(group * self.per_group, self.per_group)
        at = pl.ds(pl.multiple_of(place * rows, rows), rows)
        return pltpu.make_async_copy(
            source.at[span], self.dest.at[span, :, at, :], self.sems.at[distance, group]
        )

    def start(self, group):
        self.copy(self.own, 0, group).start()
        for distance in range(1, self.places):

            @pl.when(self.z >= distance)
            def _():
                self.copy(self.ups[distance - 1], distance, group).start()

            @pl.when(self.z < distance)
            def _():
                self.copy(self.downs[self.places - distance - 1], distance, group).start()

    def wait(self, group):
        for distance in range(self.places):
            self.copy(self.own, distance, group).wait()


NT = (((1,), (1,)), ((), ()))
NN = (((1,), (0,)), ((), ()))


def dot(a, b, dims):
    return lax.dot_general(a, b, dims, preferred_element_type=F32)


def rows_kernel(meta, own, far_a, far_b, dest, sems):
    rows, half = own.shape[0], own.shape[1] // 2
    s = meta[2]
    first = pl.ds(pl.multiple_of(s * half, half), half)
    second = pl.ds(pl.multiple_of((1 - s) * half, half), half)
    copies = (
        pltpu.make_async_copy(own, dest.at[pl.ds(0, rows)], sems.at[0]),
        pltpu.make_async_copy(far_a, dest.at[pl.ds(rows, rows), first], sems.at[1]),
        pltpu.make_async_copy(far_b, dest.at[pl.ds(rows, rows), second], sems.at[2]),
    )
    for copy in copies:
        copy.start()
    for copy in copies:
        copy.wait()


class Part:
    def __init__(self, meta, weight_refs, w, wsem, per_group, first, halves):
        self.weights = Weights(meta, weight_refs, w, wsem, per_group)
        self.w, self.per_group = w, per_group
        self.base = meta[3] + first
        self.count = w.shape[0] // halves
        self.slots, self.size = w.shape[1], w.shape[2]
        self.groups = self.count // per_group
        for group in range(self.groups):
            for half in range(halves):
                self.weights.start(half * self.groups + group)

    def lanes(self, h):
        return jnp.concatenate([self.w[h, k] for k in range(self.slots)], axis=1)

    def flat(self, h):
        return self.w[self.count + h].reshape(self.slots * self.size, self.size)

    def gathered(self, rows, lists, h):
        return jnp.concatenate(
            [rows[:, columns(lists[self.base + h, k], self.size)] for k in range(self.slots)],
            axis=1,
        )

    def add(self, sums, lists, h, values):
        for k in range(self.slots):
            at = columns(lists[self.base + h, k], self.size)
            sums[:, at] += values[:, k * self.size : (k + 1) * self.size]

    def loop(self, halves, body):
        def group_body(group, _):
            for half in range(halves):
                self.weights.wait(half * self.groups + group)
            for i in range(self.per_group):
                body(group * self.per_group + i)
            return 0

        lax.fori_loop(0, self.groups, group_body, 0)

    def middle(self, h, tok, cot, in_list, out_list):
        hidden = dot(self.gathered(tok, in_list, h), self.lanes(h), NT)
        activated, slopes = gelu_pair(hidden)
        back_act = dot(self.gathered(cot, out_list, h), self.flat(h), NN)
        return activated.astype(BF16), (back_act * slopes).astype(BF16)


def early_kernel(shards, per_group, first, meta, in_list, out_list, *refs):
    tok, cot, sums, sums_g, w, wsem = refs[shards:]
    part = Part(meta, refs[:shards], w, wsem, per_group, first, 2)
    sums[...] = jnp.zeros_like(sums)
    sums_g[...] = jnp.zeros_like(sums_g)

    def body(h):
        act, back = part.middle(h, tok, cot, in_list, out_list)
        part.add(sums, out_list, h, dot(act, part.flat(h), NT))
        part.add(sums_g, in_list, h, dot(back, part.lanes(h), NN))

    part.loop(2, body)


def split_store(meta, sums, keep, send):
    m, s = meta[1], meta[2]
    width = keep.shape[2]
    for far in range(2):
        row = 2 * (m if far == 0 else 1 - m)
        send[far] = sums[:, columns(row + 1 - s, width)].astype(BF16)
        keep[far] = sums[:, columns(row + s, width)].astype(BF16)


def late_out_kernel(shards, per_group, first, meta, in_list, out_list, *refs):
    tok, cot, _, _, _, keep, send, backs, sums, _, w, wsem = refs[shards:]
    part = Part(meta, refs[:shards], w, wsem, per_group, first, 2)

    def body(h):
        act, backs[h] = part.middle(h, tok, cot, in_list, out_list)
        part.add(sums, out_list, h, dot(act, part.flat(h), NT))

    part.loop(2, body)
    split_store(meta, sums, keep, send)


def late_grad_kernel(shards, per_group, first, meta, in_list, *refs):
    backs, _, keep, send, sums, w, wsem = refs[shards:]
    part = Part(meta, refs[:shards], w, wsem, per_group, first, 1)

    def body(h):
        part.add(sums, in_list, h, dot(backs[h], part.lanes(h), NN))

    part.loop(1, body)
    split_store(meta, sums, keep, send)


def shape(dims, dtype=BF16):
    return jax.ShapeDtypeStruct(dims, dtype)


def pinned(a):
    return pltpu.with_memory_space_constraint(a, pltpu.VMEM)


def both_rows(meta, own, far_a, far_b):
    rows, width = own.shape
    any_space, smem = (pl.BlockSpec(memory_space=m) for m in (pl.ANY, pltpu.SMEM))
    return pl.pallas_call(
        rows_kernel,
        name="both_rows",
        out_shape=pltpu.VMEM((2 * rows, width), BF16),
        in_specs=[smem] + [any_space] * 3,
        out_specs=pl.BlockSpec(memory_space=pltpu.VMEM),
        scratch_shapes=[pltpu.SemaphoreType.DMA((3,))],
        compiler_params=pltpu.CompilerParams(vmem_limit_bytes=2**20),
        cost_estimate=pl.CostEstimate(
            flops=0, bytes_accessed=4 * rows * width, transcendentals=0
        ),
    )(meta, own, far_a, far_b)


def call(kernel, name, first, halves, scalars, weights, others, outs, aliases, products):
    blocks, slots, _, size = weights[0].shape
    count = blocks // 2
    per_group = 2 if count % 2 == 0 else 1
    places = (len(weights) + 1) // 2
    hbm, smem, vmem = (pl.BlockSpec(memory_space=m) for m in (pltpu.HBM, pltpu.SMEM, pltpu.VMEM))
    skip = len(scalars) + len(weights)
    return pl.pallas_call(
        functools.partial(kernel, len(weights), per_group, first),
        name=name,
        out_shape=outs,
        in_specs=[smem] * len(scalars) + [hbm] * len(weights) + [vmem] * len(others),
        out_specs=[vmem] * len(outs),
        scratch_shapes=[
            pltpu.VMEM((halves * count, slots, size, size), BF16),
            pltpu.SemaphoreType.DMA((places, halves * count // per_group)),
        ],
        input_output_aliases={skip + i: o for i, o in aliases.items()},
        compiler_params=pltpu.CompilerParams(vmem_limit_bytes=VMEM_MIB * 2**20),
        cost_estimate=pl.CostEstimate(
            flops=products * count * size * size,
            bytes_accessed=products * count * size,
            transcendentals=0,
        ),
    )(*scalars, *weights, *[pinned(a) for a in others])


VMEM_MIB = 14


def tie(held, *names):
    values = lax.optimization_barrier(tuple(held[n] for n in names))
    held.update(zip(names, values))


LATE = 5
FAR_TIE = 2
TOK_TIE = 1
FLOPS = 3 * 10**9


def marker(held, cost, *names):
    def kernel(a, b):
        b[...] = a[...]

    tie(held, "mark", *names)
    held["mark"] = pl.pallas_call(
        kernel,
        name="marker",
        out_shape=shape(held["mark"].shape, F32),
        compiler_params=pltpu.CompilerParams(vmem_limit_bytes=2**20),
        cost_estimate=pl.CostEstimate(
            flops=cost, bytes_accessed=MARK * 2**20, transcendentals=0
        ),
    )(held["mark"])
    tie(held, "mark", *names)


MARK = 1


def hop(held, part, step, places):
    up, down = (held["%s%d%d" % (way, part, step - 1)] for way in ("up", "down"))
    with jax.named_scope("part%d_%d" % (part, step)):
        held["up%d%d" % (part, step)] = lax.ppermute(
            up, "seq", [(z, z + 1) for z in range(step - 1, places - 1)]
        )
        held["down%d%d" % (part, step)] = lax.ppermute(
            down, "seq", [(z + 1, z) for z in range(0, places - step)]
        )
    return "up%d%d" % (part, step), "down%d%d" % (part, step)


def add(a, b):
    return (a.astype(F32) + b.astype(F32)).astype(BF16)


def reduce_pair(keep, send):
    rows, width = keep.shape[1] // 2, keep.shape[2] // 2
    u = add(keep, lax.ppermute(send, "sub", SWAP))
    x_in = lax.ppermute(u[1, :, :width], "mdl", SWAP)
    y_in = lax.ppermute(u[:, rows:, width:], "grp", SWAP)
    left = add(u[0, :, :width], x_in)
    right = add(u[:, :rows, width:], y_in)
    left_in = lax.ppermute(left[rows:], "grp", SWAP)
    right_in = lax.ppermute(right[1], "mdl", SWAP)
    return jnp.concatenate([add(left[:rows], left_in), add(right[0], right_in)], axis=1)


def fast(tokens, cotangent, w_in, w_out, in_blocks, out_blocks):
    places = lax.axis_size("seq")
    model_width = tokens.shape[1]
    mine = w_in.shape[0] // 2
    counts = (6, 5, mine - 11)
    firsts = (0, 6, 11)
    grp, z, m, s = (lax.axis_index(a) for a in ("grp", "seq", "mdl", "sub"))
    meta = jnp.stack([z, m, s, grp * mine]).astype(jnp.int32)
    rows, both = tokens.shape[0], 2 * tokens.shape[0]
    counts = (mine - LATE, LATE)
    firsts = (0, mine - LATE)

    def part(first, count):
        start = (grp * mine + first, 0, 0, 0)
        size = (count,) + w_in.shape[1:]
        return jnp.concatenate([lax.dynamic_slice(w, start, size) for w in (w_in, w_out)], axis=0)

    parts = [part(f, c) for f, c in zip(firsts, counts)]
    half = model_width // 2
    tok_half, cot_half = (
        lax.dynamic_slice_in_dim(a, s * half, half, 1) for a in (tokens, cotangent)
    )
    held = {"tok_a": tok_half, "cot_a": cot_half, "mark": jnp.zeros((8, 128), F32)}
    for i, p in enumerate(parts):
        held["own%d" % i] = held["up%d0" % i] = held["down%d0" % i] = p
    order = [(i, step) for step in range(1, places) for i in range(len(parts))]
    sent = []
    for n, (i, step) in enumerate(order):
        if n == 1:
            held["tok_a"] = lax.ppermute(held["tok_a"], "grp", SWAP)
            held["cot_a"] = lax.ppermute(held["cot_a"], "grp", SWAP)
        if n >= 2:
            names = sent[n - 2]
            names += ("tok_a",) if n - 2 == TOK_TIE else ()
            names += ("cot_a",) if n - 2 == FAR_TIE else ()
            marker(held, FLOPS, *names)
        sent.append(hop(held, i, step, places))
    tok_a, cot_a = held["tok_a"], held["cot_a"]
    tok_b, cot_b = (lax.ppermute(a, "sub", SWAP) for a in (tok_a, cot_a))
    early, late = [
        [held["own%d" % i]]
        + [held["%s%d%d" % (way, i, step)] for way in ("up", "down") for step in range(1, places)]
        for i in range(len(parts))
    ]

    sums_shape = pltpu.VMEM((both, model_width), F32)
    piece = pltpu.VMEM((2, both, model_width // 4), BF16)
    row_arrays = [
        both_rows(meta, tokens, tok_a, tok_b),
        both_rows(meta, cotangent, cot_a, cot_b),
    ]
    scalars = [meta, in_blocks, out_blocks]
    size = w_in.shape[3]
    sums, sums_g = call(
        early_kernel,
        "early",
        0,
        2,
        scalars,
        early,
        row_arrays,
        [sums_shape] * 2,
        {},
        4,
    )
    keep, send, backs, _, sums_g = call(
        late_out_kernel,
        "late_out",
        firsts[1],
        2,
        scalars,
        late,
        row_arrays + [held["mark"], sums, sums_g],
        [piece, piece, pltpu.VMEM((counts[1], both, size), BF16), sums_shape, sums_shape],
        {3: 3, 4: 4},
        3,
    )
    keep_g, send_g, _ = call(
        late_grad_kernel,
        "late_grad",
        firsts[1],
        1,
        scalars[:2],
        late,
        [backs, sums_g],
        [piece, piece, sums_shape],
        {1: 2},
        1,
    )
    return reduce_pair(keep, send), reduce_pair(keep_g, send_g)


def solution(mesh):
    in_specs = (
        P(("grp", "seq"), None),
        P(("grp", "seq"), None),
        P(("mdl", "sub"), None, "seq", None),
        P(("mdl", "sub"), None, "seq", None),
        P(("mdl", "sub"), None),
        P(("mdl", "sub"), None),
    )
    out_specs = (P(("grp", "seq"), ("mdl", "sub")), P(("grp", "seq"), ("mdl", "sub")))
    sizes = tuple(mesh.shape[a] for a in ("grp", "seq", "mdl", "sub"))
    local = fast if sizes == (2, 4, 2, 2) else general
    return jax.shard_map(local, mesh=mesh, in_specs=in_specs, out_specs=out_specs, check_vma=False)
```

```python
import functools

import jax
import jax.numpy as jnp
from jax import lax
from jax.experimental import pallas as pl
from jax.experimental.pallas import tpu as pltpu
from jax.sharding import PartitionSpec as P

root_half = 0.7071067811865476
inv_root_two_pi = 0.3989422804014327
F32, BF16 = jnp.float32, jnp.bfloat16
SWAP = [(0, 1), (1, 0)]


def gelu_pair(hidden):
    normal_cdf = 0.5 * (1.0 + lax.erf(hidden * root_half))
    density = jnp.exp(-0.5 * hidden * hidden) * inv_root_two_pi
    return (hidden * normal_cdf, normal_cdf + hidden * density)


def selector(block_lists, blocks):
    flat_lists = block_lists.reshape(-1)
    return (flat_lists[:, None] == jnp.arange(blocks, dtype=jnp.int32)[None, :]).astype(F32)


def flat_terms(block_terms):
    return block_terms.reshape(block_terms.shape[0], -1, block_terms.shape[-1])


def general(tokens, cotangent, w_in, w_out, in_blocks, out_blocks):
    row_count = tokens.shape[0]
    block_size = w_in.shape[3]
    blocks = tokens.shape[1] // block_size
    token_blocks = jnp.take(tokens.reshape(row_count, blocks, block_size), in_blocks, axis=1)
    grad_blocks = jnp.take(cotangent.reshape(row_count, blocks, block_size), out_blocks, axis=1)
    pick_out = selector(out_blocks, blocks)
    pick_in = selector(in_blocks, blocks)
    full_in = lax.all_gather(w_in, "seq", axis=2, tiled=True)
    full_out = lax.all_gather(w_out, "seq", axis=2, tiled=True)
    hidden = jnp.einsum("rhki,hkji->rhj", token_blocks, full_in, preferred_element_type=F32)
    activated, slopes = gelu_pair(hidden)
    out_terms = jnp.einsum(
        "rhi,hkji->rhkj", activated.astype(BF16), full_out, preferred_element_type=F32
    )
    partial_out = jnp.einsum(
        "rsj,sc->rcj", flat_terms(out_terms), pick_out, precision=lax.Precision.HIGHEST
    ).reshape(row_count, -1)
    outputs = lax.psum_scatter(
        partial_out.astype(BF16), ("mdl", "sub"), scatter_dimension=1, tiled=True
    )
    back_act = jnp.einsum("rhkj,hkji->rhi", grad_blocks, full_out, preferred_element_type=F32)
    back_hidden = (back_act * slopes).astype(BF16)
    back_terms = jnp.einsum("rhj,hkji->rhki", back_hidden, full_in, preferred_element_type=F32)
    partial_in = jnp.einsum(
        "rsj,sc->rcj", flat_terms(back_terms), pick_in, precision=lax.Precision.HIGHEST
    ).reshape(row_count, -1)
    input_grad = lax.psum_scatter(
        partial_in.astype(BF16), ("mdl", "sub"), scatter_dimension=1, tiled=True
    )
    return (outputs, input_grad)


def columns(block, size):
    return pl.ds(pl.multiple_of(block * size, size), size)


class Weights:
    def __init__(self, meta, shards, dest, sems, per_group):
        places = (len(shards) + 1) // 2
        self.own, self.ups, self.downs = shards[0], shards[1:places], shards[places:]
        self.z, self.dest, self.sems = meta[0], dest, sems
        self.places, self.per_group = places, per_group

    def copy(self, source, distance, group):
        rows = source.shape[2]
        place = lax.rem(self.z - distance + self.places, self.places)
        span = pl.ds(group * self.per_group, self.per_group)
        at = pl.ds(pl.multiple_of(place * rows, rows), rows)
        return pltpu.make_async_copy(
            source.at[span], self.dest.at[span, :, at, :], self.sems.at[distance, group]
        )

    def start(self, group):
        self.copy(self.own, 0, group).start()
        for distance in range(1, self.places):

            @pl.when(self.z >= distance)
            def _():
                self.copy(self.ups[distance - 1], distance, group).start()

            @pl.when(self.z < distance)
            def _():
                self.copy(self.downs[self.places - distance - 1], distance, group).start()

    def wait(self, group):
        for distance in range(self.places):
            self.copy(self.own, distance, group).wait()


NT = (((1,), (1,)), ((), ()))
NN = (((1,), (0,)), ((), ()))


def dot(a, b, dims):
    return lax.dot_general(a, b, dims, preferred_element_type=F32)


def rows_kernel(meta, own, far_a, far_b, dest, sems):
    rows, half = own.shape[0], own.shape[1] // 2
    s = meta[2]
    first = pl.ds(pl.multiple_of(s * half, half), half)
    second = pl.ds(pl.multiple_of((1 - s) * half, half), half)
    copies = (
        pltpu.make_async_copy(own, dest.at[pl.ds(0, rows)], sems.at[0]),
        pltpu.make_async_copy(far_a, dest.at[pl.ds(rows, rows), first], sems.at[1]),
        pltpu.make_async_copy(far_b, dest.at[pl.ds(rows, rows), second], sems.at[2]),
    )
    for copy in copies:
        copy.start()
    for copy in copies:
        copy.wait()


class Part:
    def __init__(self, meta, weight_refs, w, wsem, per_group, first, halves):
        self.weights = Weights(meta, weight_refs, w, wsem, per_group)
        self.w, self.per_group = w, per_group
        self.base = meta[3] + first
        self.count = w.shape[0] // halves
        self.slots, self.size = w.shape[1], w.shape[2]
        self.groups = self.count // per_group
        for group in range(self.groups):
            for half in range(halves):
                self.weights.start(half * self.groups + group)

    def lanes(self, h):
        return jnp.concatenate([self.w[h, k] for k in range(self.slots)], axis=1)

    def flat(self, h):
        return self.w[self.count + h].reshape(self.slots * self.size, self.size)

    def gathered(self, rows, lists, h):
        return jnp.concatenate(
            [rows[:, columns(lists[self.base + h, k], self.size)] for k in range(self.slots)],
            axis=1,
        )

    def add(self, sums, lists, h, values):
        for k in range(self.slots):
            at = columns(lists[self.base + h, k], self.size)
            sums[:, at] += values[:, k * self.size : (k + 1) * self.size]

    def loop(self, halves, body):
        def group_body(group, _):
            for half in range(halves):
                self.weights.wait(half * self.groups + group)
            for i in range(self.per_group):
                body(group * self.per_group + i)
            return 0

        lax.fori_loop(0, self.groups, group_body, 0)

    def middle(self, h, tok, cot, in_list, out_list):
        hidden = dot(self.gathered(tok, in_list, h), self.lanes(h), NT)
        activated, slopes = gelu_pair(hidden)
        back_act = dot(self.gathered(cot, out_list, h), self.flat(h), NN)
        return activated.astype(BF16), (back_act * slopes).astype(BF16)


def early_kernel(shards, per_group, first, meta, in_list, out_list, *refs):
    tok, cot, sums, sums_g, w, wsem = refs[shards:]
    part = Part(meta, refs[:shards], w, wsem, per_group, first, 2)
    sums[...] = jnp.zeros_like(sums)
    sums_g[...] = jnp.zeros_like(sums_g)

    def body(h):
        act, back = part.middle(h, tok, cot, in_list, out_list)
        part.add(sums, out_list, h, dot(act, part.flat(h), NT))
        part.add(sums_g, in_list, h, dot(back, part.lanes(h), NN))

    part.loop(2, body)


def split_store(meta, sums, keep, send):
    m, s = meta[1], meta[2]
    width = keep.shape[2]
    for far in range(2):
        row = 2 * (m if far == 0 else 1 - m)
        send[far] = sums[:, columns(row + 1 - s, width)].astype(BF16)
        keep[far] = sums[:, columns(row + s, width)].astype(BF16)


class Held(Part):
    def __init__(self, meta, w, first):
        self.w, self.base = w, meta[3] + first
        self.count = w.shape[0] // 2
        self.slots, self.size = w.shape[1], w.shape[2]


def late_out_kernel(shards, per_group, first, meta, in_list, out_list, *refs):
    tok, _, _, _, keep, send, w, slopes, sums, _, wsem = refs[shards:]
    part = Part(meta, refs[:shards], w, wsem, per_group, first, 2)

    def body(h):
        hidden = dot(part.gathered(tok, in_list, h), part.lanes(h), NT)
        activated, slopes[h] = gelu_pair(hidden)
        part.add(sums, out_list, h, dot(activated.astype(BF16), part.flat(h), NT))

    part.loop(2, body)
    split_store(meta, sums, keep, send)


def late_back_kernel(first, meta, out_list, cot, w, slopes, backs):
    part = Held(meta, w, first)
    for h in range(part.count):
        back_act = dot(part.gathered(cot, out_list, h), part.flat(h), NN)
        backs[h] = (back_act * slopes[h]).astype(BF16)


def late_grad_kernel(first, meta, in_list, w, backs, _, keep, send, sums):
    part = Held(meta, w, first)
    for h in range(part.count):
        part.add(sums, in_list, h, dot(backs[h], part.lanes(h), NN))
    split_store(meta, sums, keep, send)


def shape(dims, dtype=BF16):
    return jax.ShapeDtypeStruct(dims, dtype)


def pinned(a):
    return pltpu.with_memory_space_constraint(a, pltpu.VMEM)


def both_rows(meta, own, far_a, far_b):
    rows, width = own.shape
    any_space, smem = (pl.BlockSpec(memory_space=m) for m in (pl.ANY, pltpu.SMEM))
    return pl.pallas_call(
        rows_kernel,
        name="both_rows",
        out_shape=pltpu.VMEM((2 * rows, width), BF16),
        in_specs=[smem] + [any_space] * 3,
        out_specs=pl.BlockSpec(memory_space=pltpu.VMEM),
        scratch_shapes=[pltpu.SemaphoreType.DMA((3,))],
        compiler_params=pltpu.CompilerParams(vmem_limit_bytes=2**20),
        cost_estimate=pl.CostEstimate(
            flops=0, bytes_accessed=4 * rows * width, transcendentals=0
        ),
    )(meta, own, far_a, far_b)


def call(kernel, name, first, scalars, weights, others, outs, aliases, scratch=()):
    blocks, slots, _, size = weights[0].shape
    count = blocks // 2
    per_group = 2 if count % 2 == 0 else 1
    places = (len(weights) + 1) // 2
    hbm, smem, vmem = (pl.BlockSpec(memory_space=m) for m in (pltpu.HBM, pltpu.SMEM, pltpu.VMEM))
    skip = len(scalars) + len(weights)
    return pl.pallas_call(
        functools.partial(kernel, len(weights), per_group, first),
        name=name,
        out_shape=outs,
        in_specs=[smem] * len(scalars) + [hbm] * len(weights) + [vmem] * len(others),
        out_specs=[vmem] * len(outs),
        scratch_shapes=[*scratch, pltpu.SemaphoreType.DMA((places, 2 * count // per_group))],
        input_output_aliases={skip + i: o for i, o in aliases.items()},
        compiler_params=pltpu.CompilerParams(vmem_limit_bytes=VMEM_MIB * 2**20),
        cost_estimate=pl.CostEstimate(
            flops=4 * count * size * size,
            bytes_accessed=4 * count * size,
            transcendentals=0,
        ),
    )(*scalars, *weights, *[pinned(a) for a in others])


def in_vmem(kernel, name, first, scalars, arrays, outs, aliases, flops):
    smem, vmem = (pl.BlockSpec(memory_space=m) for m in (pltpu.SMEM, pltpu.VMEM))
    return pl.pallas_call(
        functools.partial(kernel, first),
        name=name,
        out_shape=outs,
        in_specs=[smem] * len(scalars) + [vmem] * len(arrays),
        out_specs=[vmem] * len(outs),
        input_output_aliases={len(scalars) + i: o for i, o in aliases.items()},
        compiler_params=pltpu.CompilerParams(vmem_limit_bytes=VMEM_MIB * 2**20),
        cost_estimate=pl.CostEstimate(flops=flops, bytes_accessed=1024, transcendentals=0),
    )(*scalars, *[pinned(a) for a in arrays])


VMEM_MIB = 8


def tie(held, *names):
    values = lax.optimization_barrier(tuple(held[n] for n in names))
    held.update(zip(names, values))


LATE = 5
FAR_TIE = 2
TOK_TIE = 1
FLOPS = 3 * 10**9


def marker(held, cost, *names):
    def kernel(a, b):
        b[...] = a[...]

    tie(held, "mark", *names)
    held["mark"] = pl.pallas_call(
        kernel,
        name="marker",
        out_shape=shape(held["mark"].shape, F32),
        compiler_params=pltpu.CompilerParams(vmem_limit_bytes=2**20),
        cost_estimate=pl.CostEstimate(
            flops=cost, bytes_accessed=MARK * 2**20, transcendentals=0
        ),
    )(held["mark"])
    tie(held, "mark", *names)


MARK = 1


def hop(held, part, step, places):
    up, down = (held["%s%d%d" % (way, part, step - 1)] for way in ("up", "down"))
    with jax.named_scope("part%d_%d" % (part, step)):
        held["up%d%d" % (part, step)] = lax.ppermute(
            up, "seq", [(z, z + 1) for z in range(step - 1, places - 1)]
        )
        held["down%d%d" % (part, step)] = lax.ppermute(
            down, "seq", [(z + 1, z) for z in range(0, places - step)]
        )
    return "up%d%d" % (part, step), "down%d%d" % (part, step)


def add(a, b):
    return (a.astype(F32) + b.astype(F32)).astype(BF16)


def reduce_pair(keep, send):
    rows, width = keep.shape[1] // 2, keep.shape[2] // 2
    u = add(keep, lax.ppermute(send, "sub", SWAP))
    x_in = lax.ppermute(u[1, :, :width], "mdl", SWAP)
    y_in = lax.ppermute(u[:, rows:, width:], "grp", SWAP)
    left = add(u[0, :, :width], x_in)
    right = add(u[:, :rows, width:], y_in)
    left_in = lax.ppermute(left[rows:], "grp", SWAP)
    right_in = lax.ppermute(right[1], "mdl", SWAP)
    return jnp.concatenate([add(left[:rows], left_in), add(right[0], right_in)], axis=1)


def fast(tokens, cotangent, w_in, w_out, in_blocks, out_blocks):
    places = lax.axis_size("seq")
    model_width = tokens.shape[1]
    mine = w_in.shape[0] // 2
    counts = (6, 5, mine - 11)
    firsts = (0, 6, 11)
    grp, z, m, s = (lax.axis_index(a) for a in ("grp", "seq", "mdl", "sub"))
    meta = jnp.stack([z, m, s, grp * mine]).astype(jnp.int32)
    rows, both = tokens.shape[0], 2 * tokens.shape[0]
    counts = (mine - LATE, LATE)
    firsts = (0, mine - LATE)

    def part(first, count):
        start = (grp * mine + first, 0, 0, 0)
        size = (count,) + w_in.shape[1:]
        return jnp.concatenate([lax.dynamic_slice(w, start, size) for w in (w_in, w_out)], axis=0)

    parts = [part(f, c) for f, c in zip(firsts, counts)]
    half = model_width // 2
    tok_half, cot_half = (
        lax.dynamic_slice_in_dim(a, s * half, half, 1) for a in (tokens, cotangent)
    )
    held = {"tok_a": tok_half, "cot_a": cot_half, "mark": jnp.zeros((8, 128), F32)}
    for i, p in enumerate(parts):
        held["own%d" % i] = held["up%d0" % i] = held["down%d0" % i] = p
    order = [(i, step) for step in range(1, places) for i in range(len(parts))]
    sent = []
    for n, (i, step) in enumerate(order):
        if n == 1:
            held["tok_a"] = lax.ppermute(held["tok_a"], "grp", SWAP)
            held["cot_a"] = lax.ppermute(held["cot_a"], "grp", SWAP)
        if n >= 2:
            names = sent[n - 2]
            names += ("tok_a",) if n - 2 == TOK_TIE else ()
            names += ("cot_a",) if n - 2 == FAR_TIE else ()
            marker(held, FLOPS, *names)
        sent.append(hop(held, i, step, places))
    tok_a, cot_a = held["tok_a"], held["cot_a"]
    tok_b, cot_b = (lax.ppermute(a, "sub", SWAP) for a in (tok_a, cot_a))
    early, late = [
        [held["own%d" % i]]
        + [held["%s%d%d" % (way, i, step)] for way in ("up", "down") for step in range(1, places)]
        for i in range(len(parts))
    ]

    sums_shape = pltpu.VMEM((both, model_width), F32)
    piece = pltpu.VMEM((2, both, model_width // 4), BF16)
    row_arrays = [
        both_rows(meta, tokens, tok_a, tok_b),
        both_rows(meta, cotangent, cot_a, cot_b),
    ]
    scalars = [meta, in_blocks, out_blocks]
    size = w_in.shape[3]
    blocks_shape = w_in.shape[1:2] + (size, size)
    sums, sums_g = call(
        early_kernel,
        "early",
        0,
        scalars,
        early,
        row_arrays,
        [sums_shape] * 2,
        {},
        [pltpu.VMEM((2 * counts[0],) + blocks_shape, BF16)],
    )
    w_shape = pltpu.VMEM((2 * counts[1],) + blocks_shape, BF16)
    slopes_shape = pltpu.VMEM((counts[1], both, size), F32)
    keep, send, late_w, slopes, _, sums_g = call(
        late_out_kernel,
        "late_out",
        firsts[1],
        scalars,
        late,
        [row_arrays[0], held["mark"], sums, sums_g],
        [piece, piece, w_shape, slopes_shape, sums_shape, sums_shape],
        {2: 4, 3: 5},
    )
    (backs,) = in_vmem(
        late_back_kernel,
        "late_back",
        firsts[1],
        [meta, out_blocks],
        [row_arrays[1], late_w, slopes],
        [pltpu.VMEM((counts[1], both, size), BF16)],
        {},
        BACK_FLOPS,
    )
    keep_g, send_g, _ = in_vmem(
        late_grad_kernel,
        "late_grad",
        firsts[1],
        [meta, in_blocks],
        [late_w, backs, sums_g],
        [piece, piece, sums_shape],
        {2: 2},
        GRAD_FLOPS,
    )
    return reduce_pair(keep, send), reduce_pair(keep_g, send_g)


BACK_FLOPS = 10**9
GRAD_FLOPS = 10**9


def solution(mesh):
    in_specs = (
        P(("grp", "seq"), None),
        P(("grp", "seq"), None),
        P(("mdl", "sub"), None, "seq", None),
        P(("mdl", "sub"), None, "seq", None),
        P(("mdl", "sub"), None),
        P(("mdl", "sub"), None),
    )
    out_specs = (P(("grp", "seq"), ("mdl", "sub")), P(("grp", "seq"), ("mdl", "sub")))
    sizes = tuple(mesh.shape[a] for a in ("grp", "seq", "mdl", "sub"))
    local = fast if sizes == (2, 4, 2, 2) else general
    return jax.shard_map(local, mesh=mesh, in_specs=in_specs, out_specs=out_specs, check_vma=False)
```

```python
import functools

import jax
import jax.numpy as jnp
from jax import lax
from jax.experimental import pallas as pl
from jax.experimental.pallas import tpu as pltpu
from jax.sharding import PartitionSpec as P

root_half = 0.7071067811865476
inv_root_two_pi = 0.3989422804014327
F32, BF16 = jnp.float32, jnp.bfloat16
SWAP = [(0, 1), (1, 0)]


def gelu_pair(hidden):
    normal_cdf = 0.5 * (1.0 + lax.erf(hidden * root_half))
    density = jnp.exp(-0.5 * hidden * hidden) * inv_root_two_pi
    return (hidden * normal_cdf, normal_cdf + hidden * density)


def selector(block_lists, blocks):
    flat_lists = block_lists.reshape(-1)
    return (flat_lists[:, None] == jnp.arange(blocks, dtype=jnp.int32)[None, :]).astype(F32)


def flat_terms(block_terms):
    return block_terms.reshape(block_terms.shape[0], -1, block_terms.shape[-1])


def general(tokens, cotangent, w_in, w_out, in_blocks, out_blocks):
    row_count = tokens.shape[0]
    block_size = w_in.shape[3]
    blocks = tokens.shape[1] // block_size
    token_blocks = jnp.take(tokens.reshape(row_count, blocks, block_size), in_blocks, axis=1)
    grad_blocks = jnp.take(cotangent.reshape(row_count, blocks, block_size), out_blocks, axis=1)
    pick_out = selector(out_blocks, blocks)
    pick_in = selector(in_blocks, blocks)
    full_in = lax.all_gather(w_in, "seq", axis=2, tiled=True)
    full_out = lax.all_gather(w_out, "seq", axis=2, tiled=True)
    hidden = jnp.einsum("rhki,hkji->rhj", token_blocks, full_in, preferred_element_type=F32)
    activated, slopes = gelu_pair(hidden)
    out_terms = jnp.einsum(
        "rhi,hkji->rhkj", activated.astype(BF16), full_out, preferred_element_type=F32
    )
    partial_out = jnp.einsum(
        "rsj,sc->rcj", flat_terms(out_terms), pick_out, precision=lax.Precision.HIGHEST
    ).reshape(row_count, -1)
    outputs = lax.psum_scatter(
        partial_out.astype(BF16), ("mdl", "sub"), scatter_dimension=1, tiled=True
    )
    back_act = jnp.einsum("rhkj,hkji->rhi", grad_blocks, full_out, preferred_element_type=F32)
    back_hidden = (back_act * slopes).astype(BF16)
    back_terms = jnp.einsum("rhj,hkji->rhki", back_hidden, full_in, preferred_element_type=F32)
    partial_in = jnp.einsum(
        "rsj,sc->rcj", flat_terms(back_terms), pick_in, precision=lax.Precision.HIGHEST
    ).reshape(row_count, -1)
    input_grad = lax.psum_scatter(
        partial_in.astype(BF16), ("mdl", "sub"), scatter_dimension=1, tiled=True
    )
    return (outputs, input_grad)


def columns(block, size):
    return pl.ds(pl.multiple_of(block * size, size), size)


class Weights:
    def __init__(self, meta, shards, dest, sems, per_group):
        places = (len(shards) + 1) // 2
        self.own, self.ups, self.downs = shards[0], shards[1:places], shards[places:]
        self.z, self.dest, self.sems = meta[0], dest, sems
        self.places, self.per_group = places, per_group

    def copy(self, source, distance, group):
        rows = source.shape[2]
        place = lax.rem(self.z - distance + self.places, self.places)
        span = pl.ds(group * self.per_group, self.per_group)
        at = pl.ds(pl.multiple_of(place * rows, rows), rows)
        return pltpu.make_async_copy(
            source.at[span], self.dest.at[span, :, at, :], self.sems.at[distance, group]
        )

    def start(self, group):
        self.copy(self.own, 0, group).start()
        for distance in range(1, self.places):

            @pl.when(self.z >= distance)
            def _():
                self.copy(self.ups[distance - 1], distance, group).start()

            @pl.when(self.z < distance)
            def _():
                self.copy(self.downs[self.places - distance - 1], distance, group).start()

    def wait(self, group):
        for distance in range(self.places):
            self.copy(self.own, distance, group).wait()


NT = (((1,), (1,)), ((), ()))
NN = (((1,), (0,)), ((), ()))


def dot(a, b, dims):
    return lax.dot_general(a, b, dims, preferred_element_type=F32)


def in_hbm(a):
    return pltpu.with_memory_space_constraint(a, pltpu.HBM)


def laid_kernel(mine, first, count, w_in, w_out, dest, sems):
    start = lax.axis_index("grp") * mine + first
    copies = [
        pltpu.make_async_copy(
            w.at[pl.ds(start, count)], dest.at[pl.ds(i * count, count)], sems.at[i]
        )
        for i, w in enumerate((w_in, w_out))
    ]
    for copy in copies:
        copy.start()
    for copy in copies:
        copy.wait()


def laid_together(w_in, w_out, mine, first, count):
    return pl.pallas_call(
        functools.partial(laid_kernel, mine, first, count),
        name="laid_together",
        out_shape=pltpu.VMEM((2 * count,) + w_in.shape[1:], BF16),
        in_specs=[pl.BlockSpec(memory_space=pltpu.HBM)] * 2,
        out_specs=pl.BlockSpec(memory_space=pltpu.VMEM),
        scratch_shapes=[pltpu.SemaphoreType.DMA((2,))],
        compiler_params=pltpu.CompilerParams(vmem_limit_bytes=2**20),
        cost_estimate=pl.CostEstimate(flops=0, bytes_accessed=2**20, transcendentals=0),
    )(in_hbm(w_in), in_hbm(w_out))


def rows_kernel(meta, own, far_a, far_b, dest, sems):
    rows, half = own.shape[0], own.shape[1] // 2
    s = meta[2]
    first = pl.ds(pl.multiple_of(s * half, half), half)
    second = pl.ds(pl.multiple_of((1 - s) * half, half), half)
    copies = (
        pltpu.make_async_copy(own, dest.at[pl.ds(0, rows)], sems.at[0]),
        pltpu.make_async_copy(far_a, dest.at[pl.ds(rows, rows), first], sems.at[1]),
        pltpu.make_async_copy(far_b, dest.at[pl.ds(rows, rows), second], sems.at[2]),
    )
    for copy in copies:
        copy.start()
    for copy in copies:
        copy.wait()


class Part:
    def __init__(self, meta, weight_refs, w, wsem, per_group, first, halves):
        self.weights = Weights(meta, weight_refs, w, wsem, per_group)
        self.w, self.per_group = w, per_group
        self.base = meta[3] + first
        self.count = w.shape[0] // halves
        self.slots, self.size = w.shape[1], w.shape[2]
        self.groups = self.count // per_group
        for group in range(self.groups):
            for half in range(halves):
                self.weights.start(half * self.groups + group)

    def lanes(self, h):
        return jnp.concatenate([self.w[h, k] for k in range(self.slots)], axis=1)

    def flat(self, h):
        return self.w[self.count + h].reshape(self.slots * self.size, self.size)

    def gathered(self, rows, lists, h):
        return jnp.concatenate(
            [rows[:, columns(lists[self.base + h, k], self.size)] for k in range(self.slots)],
            axis=1,
        )

    def add(self, sums, lists, h, values):
        for k in range(self.slots):
            at = columns(lists[self.base + h, k], self.size)
            sums[:, at] += values[:, k * self.size : (k + 1) * self.size]

    def loop(self, halves, body):
        def group_body(group, _):
            for half in range(halves):
                self.weights.wait(half * self.groups + group)
            for i in range(self.per_group):
                body(group * self.per_group + i)
            return 0

        lax.fori_loop(0, self.groups, group_body, 0)

    def middle(self, h, tok, cot, in_list, out_list):
        hidden = dot(self.gathered(tok, in_list, h), self.lanes(h), NT)
        activated, slopes = gelu_pair(hidden)
        back_act = dot(self.gathered(cot, out_list, h), self.flat(h), NN)
        return activated.astype(BF16), (back_act * slopes).astype(BF16)


def early_kernel(shards, per_group, first, meta, in_list, out_list, *refs):
    tok, cot, sums, sums_g, w, wsem = refs[shards:]
    part = Part(meta, refs[:shards], w, wsem, per_group, first, 2)
    sums[...] = jnp.zeros_like(sums)
    sums_g[...] = jnp.zeros_like(sums_g)

    def body(h):
        act, back = part.middle(h, tok, cot, in_list, out_list)
        part.add(sums, out_list, h, dot(act, part.flat(h), NT))
        part.add(sums_g, in_list, h, dot(back, part.lanes(h), NN))

    part.loop(2, body)


def split_store(meta, sums, keep, send):
    m, s = meta[1], meta[2]
    width = keep.shape[2]
    for far in range(2):
        row = 2 * (m if far == 0 else 1 - m)
        send[far] = sums[:, columns(row + 1 - s, width)].astype(BF16)
        keep[far] = sums[:, columns(row + s, width)].astype(BF16)


class Held(Part):
    def __init__(self, meta, w, first):
        self.w, self.base = w, meta[3] + first
        self.count = w.shape[0] // 2
        self.slots, self.size = w.shape[1], w.shape[2]


def late_out_kernel(shards, per_group, first, meta, in_list, out_list, *refs):
    tok, _, _, _, keep, send, w, slopes, sums, _, wsem = refs[shards:]
    part = Part(meta, refs[:shards], w, wsem, per_group, first, 2)

    def body(h):
        hidden = dot(part.gathered(tok, in_list, h), part.lanes(h), NT)
        activated, slopes[h] = gelu_pair(hidden)
        part.add(sums, out_list, h, dot(activated.astype(BF16), part.flat(h), NT))

    part.loop(2, body)
    split_store(meta, sums, keep, send)


def late_back_kernel(first, meta, out_list, cot, w, slopes, backs):
    part = Held(meta, w, first)
    for h in range(part.count):
        back_act = dot(part.gathered(cot, out_list, h), part.flat(h), NN)
        backs[h] = (back_act * slopes[h]).astype(BF16)


def late_grad_kernel(first, meta, in_list, w, backs, _, keep, send, sums):
    part = Held(meta, w, first)
    for h in range(part.count):
        part.add(sums, in_list, h, dot(backs[h], part.lanes(h), NN))
    split_store(meta, sums, keep, send)


def shape(dims, dtype=BF16):
    return jax.ShapeDtypeStruct(dims, dtype)


def pinned(a):
    return pltpu.with_memory_space_constraint(a, pltpu.VMEM)


def both_rows(meta, own, far_a, far_b):
    rows, width = own.shape
    any_space, smem = (pl.BlockSpec(memory_space=m) for m in (pl.ANY, pltpu.SMEM))
    return pl.pallas_call(
        rows_kernel,
        name="both_rows",
        out_shape=pltpu.VMEM((2 * rows, width), BF16),
        in_specs=[smem] + [any_space] * 3,
        out_specs=pl.BlockSpec(memory_space=pltpu.VMEM),
        scratch_shapes=[pltpu.SemaphoreType.DMA((3,))],
        compiler_params=pltpu.CompilerParams(vmem_limit_bytes=2**20),
        cost_estimate=pl.CostEstimate(
            flops=0, bytes_accessed=4 * rows * width, transcendentals=0
        ),
    )(meta, *[in_hbm(a) for a in (own, far_a, far_b)])


def call(kernel, name, first, scalars, weights, others, outs, aliases, scratch=()):
    blocks, slots, _, size = weights[0].shape
    count = blocks // 2
    per_group = 2 if count % 2 == 0 else 1
    places = (len(weights) + 1) // 2
    hbm, smem, vmem = (pl.BlockSpec(memory_space=m) for m in (pltpu.HBM, pltpu.SMEM, pltpu.VMEM))
    skip = len(scalars) + len(weights)
    return pl.pallas_call(
        functools.partial(kernel, len(weights), per_group, first),
        name=name,
        out_shape=outs,
        in_specs=[smem] * len(scalars) + [hbm] * len(weights) + [vmem] * len(others),
        out_specs=[vmem] * len(outs),
        scratch_shapes=[*scratch, pltpu.SemaphoreType.DMA((places, 2 * count // per_group))],
        input_output_aliases={skip + i: o for i, o in aliases.items()},
        compiler_params=pltpu.CompilerParams(vmem_limit_bytes=VMEM_MIB * 2**20),
        cost_estimate=pl.CostEstimate(
            flops=4 * count * size * size,
            bytes_accessed=4 * count * size,
            transcendentals=0,
        ),
    )(*scalars, *[in_hbm(a) for a in weights], *[pinned(a) for a in others])


def in_vmem(kernel, name, first, scalars, arrays, outs, aliases, flops):
    smem, vmem = (pl.BlockSpec(memory_space=m) for m in (pltpu.SMEM, pltpu.VMEM))
    return pl.pallas_call(
        functools.partial(kernel, first),
        name=name,
        out_shape=outs,
        in_specs=[smem] * len(scalars) + [vmem] * len(arrays),
        out_specs=[vmem] * len(outs),
        input_output_aliases={len(scalars) + i: o for i, o in aliases.items()},
        compiler_params=pltpu.CompilerParams(vmem_limit_bytes=VMEM_MIB * 2**20),
        cost_estimate=pl.CostEstimate(flops=flops, bytes_accessed=1024, transcendentals=0),
    )(*scalars, *[pinned(a) for a in arrays])


VMEM_MIB = 8


def tie(held, *names):
    values = lax.optimization_barrier(tuple(held[n] for n in names))
    held.update(zip(names, values))


LATE = 5
FAR_TIE = 2
TOK_TIE = 1
FLOPS = 3 * 10**9


def marker(held, cost, *names):
    def kernel(a, b):
        b[...] = a[...]

    tie(held, "mark", *names)
    held["mark"] = pl.pallas_call(
        kernel,
        name="marker",
        out_shape=shape(held["mark"].shape, F32),
        compiler_params=pltpu.CompilerParams(vmem_limit_bytes=2**20),
        cost_estimate=pl.CostEstimate(
            flops=cost, bytes_accessed=MARK * 2**20, transcendentals=0
        ),
    )(held["mark"])
    tie(held, "mark", *names)


MARK = 1


def hop(held, part, step, places):
    up, down = (held["%s%d%d" % (way, part, step - 1)] for way in ("up", "down"))
    with jax.named_scope("part%d_%d" % (part, step)):
        held["up%d%d" % (part, step)] = lax.ppermute(
            up, "seq", [(z, z + 1) for z in range(step - 1, places - 1)]
        )
        held["down%d%d" % (part, step)] = lax.ppermute(
            down, "seq", [(z + 1, z) for z in range(0, places - step)]
        )
    return "up%d%d" % (part, step), "down%d%d" % (part, step)


def add(a, b):
    return (a.astype(F32) + b.astype(F32)).astype(BF16)


def reduce_pair(keep, send):
    rows, width = keep.shape[1] // 2, keep.shape[2] // 2
    u = add(keep, lax.ppermute(send, "sub", SWAP))
    x_in = lax.ppermute(u[1, :, :width], "mdl", SWAP)
    y_in = lax.ppermute(u[:, rows:, width:], "grp", SWAP)
    left = add(u[0, :, :width], x_in)
    right = add(u[:, :rows, width:], y_in)
    left_in = lax.ppermute(left[rows:], "grp", SWAP)
    right_in = lax.ppermute(right[1], "mdl", SWAP)
    return jnp.concatenate([add(left[:rows], left_in), add(right[0], right_in)], axis=1)


def fast(tokens, cotangent, w_in, w_out, in_blocks, out_blocks):
    places = lax.axis_size("seq")
    model_width = tokens.shape[1]
    mine = w_in.shape[0] // 2
    counts = (6, 5, mine - 11)
    firsts = (0, 6, 11)
    grp, z, m, s = (lax.axis_index(a) for a in ("grp", "seq", "mdl", "sub"))
    meta = jnp.stack([z, m, s, grp * mine]).astype(jnp.int32)
    rows, both = tokens.shape[0], 2 * tokens.shape[0]
    counts = (mine - LATE, LATE)
    firsts = (0, mine - LATE)

    def part(first, count):
        return laid_together(w_in, w_out, mine, first, count)

    parts = [part(f, c) for f, c in zip(firsts, counts)]
    half = model_width // 2
    tok_half, cot_half = (
        lax.dynamic_slice_in_dim(a, s * half, half, 1) for a in (tokens, cotangent)
    )
    held = {"tok_a": tok_half, "cot_a": cot_half, "mark": jnp.zeros((8, 128), F32)}
    for i, p in enumerate(parts):
        held["own%d" % i] = held["up%d0" % i] = held["down%d0" % i] = p
    order = [(i, step) for step in range(1, places) for i in range(len(parts))]
    sent = []
    for n, (i, step) in enumerate(order):
        if n == 1:
            held["tok_a"] = lax.ppermute(held["tok_a"], "grp", SWAP)
            held["cot_a"] = lax.ppermute(held["cot_a"], "grp", SWAP)
        if n >= 2:
            names = sent[n - 2]
            names += ("tok_a",) if n - 2 == TOK_TIE else ()
            names += ("cot_a",) if n - 2 == FAR_TIE else ()
            marker(held, FLOPS, *names)
        sent.append(hop(held, i, step, places))
    tok_a, cot_a = held["tok_a"], held["cot_a"]
    tok_b, cot_b = (lax.ppermute(a, "sub", SWAP) for a in (tok_a, cot_a))
    early, late = [
        [held["own%d" % i]]
        + [held["%s%d%d" % (way, i, step)] for way in ("up", "down") for step in range(1, places)]
        for i in range(len(parts))
    ]

    sums_shape = pltpu.VMEM((both, model_width), F32)
    piece = pltpu.VMEM((2, both, model_width // 4), BF16)
    row_arrays = [
        both_rows(meta, tokens, tok_a, tok_b),
        both_rows(meta, cotangent, cot_a, cot_b),
    ]
    scalars = [meta, in_blocks, out_blocks]
    size = w_in.shape[3]
    blocks_shape = w_in.shape[1:2] + (size, size)
    sums, sums_g = call(
        early_kernel,
        "early",
        0,
        scalars,
        early,
        row_arrays,
        [sums_shape] * 2,
        {},
        [pltpu.VMEM((2 * counts[0],) + blocks_shape, BF16)],
    )
    w_shape = pltpu.VMEM((2 * counts[1],) + blocks_shape, BF16)
    slopes_shape = pltpu.VMEM((counts[1], both, size), F32)
    keep, send, late_w, slopes, _, sums_g = call(
        late_out_kernel,
        "late_out",
        firsts[1],
        scalars,
        late,
        [row_arrays[0], held["mark"], sums, sums_g],
        [piece, piece, w_shape, slopes_shape, sums_shape, sums_shape],
        {2: 4, 3: 5},
    )
    (backs,) = in_vmem(
        late_back_kernel,
        "late_back",
        firsts[1],
        [meta, out_blocks],
        [row_arrays[1], late_w, slopes],
        [pltpu.VMEM((counts[1], both, size), BF16)],
        {},
        BACK_FLOPS,
    )
    keep_g, send_g, _ = in_vmem(
        late_grad_kernel,
        "late_grad",
        firsts[1],
        [meta, in_blocks],
        [late_w, backs, sums_g],
        [piece, piece, sums_shape],
        {2: 2},
        GRAD_FLOPS,
    )
    return reduce_pair(keep, send), reduce_pair(keep_g, send_g)


BACK_FLOPS = 10**9
GRAD_FLOPS = 10**9


def solution(mesh):
    in_specs = (
        P(("grp", "seq"), None),
        P(("grp", "seq"), None),
        P(("mdl", "sub"), None, "seq", None),
        P(("mdl", "sub"), None, "seq", None),
        P(("mdl", "sub"), None),
        P(("mdl", "sub"), None),
    )
    out_specs = (P(("grp", "seq"), ("mdl", "sub")), P(("grp", "seq"), ("mdl", "sub")))
    sizes = tuple(mesh.shape[a] for a in ("grp", "seq", "mdl", "sub"))
    local = fast if sizes == (2, 4, 2, 2) else general
    return jax.shard_map(local, mesh=mesh, in_specs=in_specs, out_specs=out_specs, check_vma=False)
```

```python
import functools

import jax
import jax.numpy as jnp
from jax import lax
from jax.experimental import pallas as pl
from jax.experimental.pallas import tpu as pltpu
from jax.sharding import PartitionSpec as P

root_half = 0.7071067811865476
inv_root_two_pi = 0.3989422804014327
F32, BF16 = jnp.float32, jnp.bfloat16
SWAP = [(0, 1), (1, 0)]


def gelu_pair(hidden):
    normal_cdf = 0.5 * (1.0 + lax.erf(hidden * root_half))
    density = jnp.exp(-0.5 * hidden * hidden) * inv_root_two_pi
    return (hidden * normal_cdf, normal_cdf + hidden * density)


def selector(block_lists, blocks):
    flat_lists = block_lists.reshape(-1)
    return (flat_lists[:, None] == jnp.arange(blocks, dtype=jnp.int32)[None, :]).astype(F32)


def flat_terms(block_terms):
    return block_terms.reshape(block_terms.shape[0], -1, block_terms.shape[-1])


def general(tokens, cotangent, w_in, w_out, in_blocks, out_blocks):
    row_count = tokens.shape[0]
    block_size = w_in.shape[3]
    blocks = tokens.shape[1] // block_size
    token_blocks = jnp.take(tokens.reshape(row_count, blocks, block_size), in_blocks, axis=1)
    grad_blocks = jnp.take(cotangent.reshape(row_count, blocks, block_size), out_blocks, axis=1)
    pick_out = selector(out_blocks, blocks)
    pick_in = selector(in_blocks, blocks)
    full_in = lax.all_gather(w_in, "seq", axis=2, tiled=True)
    full_out = lax.all_gather(w_out, "seq", axis=2, tiled=True)
    hidden = jnp.einsum("rhki,hkji->rhj", token_blocks, full_in, preferred_element_type=F32)
    activated, slopes = gelu_pair(hidden)
    out_terms = jnp.einsum(
        "rhi,hkji->rhkj", activated.astype(BF16), full_out, preferred_element_type=F32
    )
    partial_out = jnp.einsum(
        "rsj,sc->rcj", flat_terms(out_terms), pick_out, precision=lax.Precision.HIGHEST
    ).reshape(row_count, -1)
    outputs = lax.psum_scatter(
        partial_out.astype(BF16), ("mdl", "sub"), scatter_dimension=1, tiled=True
    )
    back_act = jnp.einsum("rhkj,hkji->rhi", grad_blocks, full_out, preferred_element_type=F32)
    back_hidden = (back_act * slopes).astype(BF16)
    back_terms = jnp.einsum("rhj,hkji->rhki", back_hidden, full_in, preferred_element_type=F32)
    partial_in = jnp.einsum(
        "rsj,sc->rcj", flat_terms(back_terms), pick_in, precision=lax.Precision.HIGHEST
    ).reshape(row_count, -1)
    input_grad = lax.psum_scatter(
        partial_in.astype(BF16), ("mdl", "sub"), scatter_dimension=1, tiled=True
    )
    return (outputs, input_grad)


def columns(block, size):
    return pl.ds(pl.multiple_of(block * size, size), size)


class Weights:
    def __init__(self, meta, shards, dest, sems, per_group):
        places = (len(shards) + 1) // 2
        self.own, self.ups, self.downs = shards[0], shards[1:places], shards[places:]
        self.z, self.dest, self.sems = meta[0], dest, sems
        self.places, self.per_group = places, per_group

    def copy(self, source, distance, group):
        rows = source.shape[2]
        place = lax.rem(self.z - distance + self.places, self.places)
        span = pl.ds(group * self.per_group, self.per_group)
        at = pl.ds(pl.multiple_of(place * rows, rows), rows)
        return pltpu.make_async_copy(
            source.at[span], self.dest.at[span, :, at, :], self.sems.at[distance, group]
        )

    def start(self, group):
        self.copy(self.own, 0, group).start()
        for distance in range(1, self.places):

            @pl.when(self.z >= distance)
            def _():
                self.copy(self.ups[distance - 1], distance, group).start()

            @pl.when(self.z < distance)
            def _():
                self.copy(self.downs[self.places - distance - 1], distance, group).start()

    def wait(self, group):
        for distance in range(self.places):
            self.copy(self.own, distance, group).wait()


NT = (((1,), (1,)), ((), ()))
NN = (((1,), (0,)), ((), ()))


def dot(a, b, dims):
    return lax.dot_general(a, b, dims, preferred_element_type=F32)


def rows_kernel(meta, own, far_a, far_b, dest, sums, sems):
    rows, half = own.shape[0], own.shape[1] // 2
    s = meta[2]
    first = pl.ds(pl.multiple_of(s * half, half), half)
    second = pl.ds(pl.multiple_of((1 - s) * half, half), half)
    copies = (
        pltpu.make_async_copy(own, dest.at[pl.ds(0, rows)], sems.at[0]),
        pltpu.make_async_copy(far_a, dest.at[pl.ds(rows, rows), first], sems.at[1]),
        pltpu.make_async_copy(far_b, dest.at[pl.ds(rows, rows), second], sems.at[2]),
    )
    for copy in copies:
        copy.start()
    sums[...] = jnp.zeros_like(sums)
    for copy in copies:
        copy.wait()


class Part:
    def __init__(self, meta, weight_refs, w, wsem, per_group, first, halves):
        self.weights = Weights(meta, weight_refs, w, wsem, per_group)
        self.w, self.per_group = w, per_group
        self.base = meta[3] + first
        self.count = w.shape[0] // halves
        self.slots, self.size = w.shape[1], w.shape[2]
        self.groups = self.count // per_group
        for group in range(self.groups):
            for half in range(halves):
                self.weights.start(half * self.groups + group)

    def lanes(self, h):
        return jnp.concatenate([self.w[h, k] for k in range(self.slots)], axis=1)

    def flat(self, h):
        return self.w[self.count + h].reshape(self.slots * self.size, self.size)

    def gathered(self, rows, lists, h):
        return jnp.concatenate(
            [rows[:, columns(lists[self.base + h, k], self.size)] for k in range(self.slots)],
            axis=1,
        )

    def add(self, sums, lists, h, values):
        for k in range(self.slots):
            at = columns(lists[self.base + h, k], self.size)
            sums[:, at] += values[:, k * self.size : (k + 1) * self.size]

    def loop(self, halves, body):
        def group_body(group, _):
            for half in range(halves):
                self.weights.wait(half * self.groups + group)
            for i in range(self.per_group):
                body(group * self.per_group + i)
            return 0

        lax.fori_loop(0, self.groups, group_body, 0)

    def middle(self, h, tok, cot, in_list, out_list):
        hidden = dot(self.gathered(tok, in_list, h), self.lanes(h), NT)
        activated, slopes = gelu_pair(hidden)
        back_act = dot(self.gathered(cot, out_list, h), self.flat(h), NN)
        return activated.astype(BF16), (back_act * slopes).astype(BF16)


def early_kernel(shards, per_group, first, meta, in_list, out_list, *refs):
    tok, cot, _, _, sums, sums_g, w, wsem = refs[shards:]
    part = Part(meta, refs[:shards], w, wsem, per_group, first, 2)

    def body(h):
        act, back = part.middle(h, tok, cot, in_list, out_list)
        part.add(sums, out_list, h, dot(act, part.flat(h), NT))
        part.add(sums_g, in_list, h, dot(back, part.lanes(h), NN))

    part.loop(2, body)


def split_store(meta, sums, keep, send):
    m, s = meta[1], meta[2]
    width = keep.shape[2]
    for far in range(2):
        row = 2 * (m if far == 0 else 1 - m)
        send[far] = sums[:, columns(row + 1 - s, width)].astype(BF16)
        keep[far] = sums[:, columns(row + s, width)].astype(BF16)


class Held(Part):
    def __init__(self, meta, w, first):
        self.w, self.base = w, meta[3] + first
        self.count = w.shape[0] // 2
        self.slots, self.size = w.shape[1], w.shape[2]


def late_out_kernel(shards, per_group, first, meta, in_list, out_list, *refs):
    tok, _, _, _, keep, send, w, slopes, sums, _, wsem = refs[shards:]
    part = Part(meta, refs[:shards], w, wsem, per_group, first, 2)

    def body(h):
        hidden = dot(part.gathered(tok, in_list, h), part.lanes(h), NT)
        activated, slopes[h] = gelu_pair(hidden)
        part.add(sums, out_list, h, dot(activated.astype(BF16), part.flat(h), NT))

    part.loop(2, body)
    split_store(meta, sums, keep, send)


def late_back_kernel(first, meta, out_list, cot, w, slopes, backs):
    part = Held(meta, w, first)
    for h in range(part.count):
        back_act = dot(part.gathered(cot, out_list, h), part.flat(h), NN)
        backs[h] = (back_act * slopes[h]).astype(BF16)


def late_grad_kernel(first, meta, in_list, w, backs, _, keep, send, sums):
    part = Held(meta, w, first)
    for h in range(part.count):
        part.add(sums, in_list, h, dot(backs[h], part.lanes(h), NN))
    split_store(meta, sums, keep, send)


def shape(dims, dtype=BF16):
    return jax.ShapeDtypeStruct(dims, dtype)


def pinned(a):
    return pltpu.with_memory_space_constraint(a, pltpu.VMEM)


def both_rows(meta, own, far_a, far_b):
    rows, width = own.shape
    any_space, smem = (pl.BlockSpec(memory_space=m) for m in (pl.ANY, pltpu.SMEM))
    return pl.pallas_call(
        rows_kernel,
        name="both_rows",
        out_shape=[pltpu.VMEM((2 * rows, width), t) for t in (BF16, F32)],
        in_specs=[smem] + [any_space] * 3,
        out_specs=[pl.BlockSpec(memory_space=pltpu.VMEM)] * 2,
        scratch_shapes=[pltpu.SemaphoreType.DMA((3,))],
        compiler_params=pltpu.CompilerParams(vmem_limit_bytes=2**20),
        cost_estimate=pl.CostEstimate(
            flops=0, bytes_accessed=4 * rows * width, transcendentals=0
        ),
    )(meta, own, far_a, far_b)


def call(kernel, name, first, scalars, weights, others, outs, aliases, scratch=()):
    blocks, slots, _, size = weights[0].shape
    count = blocks // 2
    per_group = 2 if count % 2 == 0 else 1
    places = (len(weights) + 1) // 2
    hbm, smem, vmem = (pl.BlockSpec(memory_space=m) for m in (pltpu.HBM, pltpu.SMEM, pltpu.VMEM))
    skip = len(scalars) + len(weights)
    return pl.pallas_call(
        functools.partial(kernel, len(weights), per_group, first),
        name=name,
        out_shape=outs,
        in_specs=[smem] * len(scalars) + [hbm] * len(weights) + [vmem] * len(others),
        out_specs=[vmem] * len(outs),
        scratch_shapes=[*scratch, pltpu.SemaphoreType.DMA((places, 2 * count // per_group))],
        input_output_aliases={skip + i: o for i, o in aliases.items()},
        compiler_params=pltpu.CompilerParams(vmem_limit_bytes=VMEM_MIB * 2**20),
        cost_estimate=pl.CostEstimate(
            flops=4 * count * size * size,
            bytes_accessed=4 * count * size,
            transcendentals=0,
        ),
    )(*scalars, *weights, *[pinned(a) for a in others])


def in_vmem(kernel, name, first, scalars, arrays, outs, aliases, flops):
    smem, vmem = (pl.BlockSpec(memory_space=m) for m in (pltpu.SMEM, pltpu.VMEM))
    return pl.pallas_call(
        functools.partial(kernel, first),
        name=name,
        out_shape=outs,
        in_specs=[smem] * len(scalars) + [vmem] * len(arrays),
        out_specs=[vmem] * len(outs),
        input_output_aliases={len(scalars) + i: o for i, o in aliases.items()},
        compiler_params=pltpu.CompilerParams(vmem_limit_bytes=VMEM_MIB * 2**20),
        cost_estimate=pl.CostEstimate(flops=flops, bytes_accessed=1024, transcendentals=0),
    )(*scalars, *[pinned(a) for a in arrays])


VMEM_MIB = 8


def tie(held, *names):
    values = lax.optimization_barrier(tuple(held[n] for n in names))
    held.update(zip(names, values))


LATE = 5
FAR_TIE = 2
TOK_TIE = 1
FLOPS = 3 * 10**9


def marker(held, cost, *names):
    def kernel(a, b):
        b[...] = a[...]

    tie(held, "mark", *names)
    held["mark"] = pl.pallas_call(
        kernel,
        name="marker",
        out_shape=shape(held["mark"].shape, F32),
        compiler_params=pltpu.CompilerParams(vmem_limit_bytes=2**20),
        cost_estimate=pl.CostEstimate(
            flops=cost, bytes_accessed=MARK * 2**20, transcendentals=0
        ),
    )(held["mark"])
    tie(held, "mark", *names)


MARK = 1


def hop(held, part, step, places):
    up, down = (held["%s%d%d" % (way, part, step - 1)] for way in ("up", "down"))
    with jax.named_scope("part%d_%d" % (part, step)):
        held["up%d%d" % (part, step)] = lax.ppermute(
            up, "seq", [(z, z + 1) for z in range(step - 1, places - 1)]
        )
        held["down%d%d" % (part, step)] = lax.ppermute(
            down, "seq", [(z + 1, z) for z in range(0, places - step)]
        )
    return "up%d%d" % (part, step), "down%d%d" % (part, step)


def add(a, b):
    return (a.astype(F32) + b.astype(F32)).astype(BF16)


def reduce_pair(keep, send):
    rows, width = keep.shape[1] // 2, keep.shape[2] // 2
    u = add(keep, lax.ppermute(send, "sub", SWAP))
    x_in = lax.ppermute(u[1, :, :width], "mdl", SWAP)
    y_in = lax.ppermute(u[:, rows:, width:], "grp", SWAP)
    left = add(u[0, :, :width], x_in)
    right = add(u[:, :rows, width:], y_in)
    left_in = lax.ppermute(left[rows:], "grp", SWAP)
    right_in = lax.ppermute(right[1], "mdl", SWAP)
    return jnp.concatenate([add(left[:rows], left_in), add(right[0], right_in)], axis=1)


def fast(tokens, cotangent, w_in, w_out, in_blocks, out_blocks):
    places = lax.axis_size("seq")
    model_width = tokens.shape[1]
    mine = w_in.shape[0] // 2
    counts = (6, 5, mine - 11)
    firsts = (0, 6, 11)
    grp, z, m, s = (lax.axis_index(a) for a in ("grp", "seq", "mdl", "sub"))
    meta = jnp.stack([z, m, s, grp * mine]).astype(jnp.int32)
    rows, both = tokens.shape[0], 2 * tokens.shape[0]
    counts = (mine - LATE, LATE)
    firsts = (0, mine - LATE)

    def part(first, count):
        start = (grp * mine + first, 0, 0, 0)
        size = (count,) + w_in.shape[1:]
        return jnp.concatenate([lax.dynamic_slice(w, start, size) for w in (w_in, w_out)], axis=0)

    parts = [part(f, c) for f, c in zip(firsts, counts)]
    half = model_width // 2
    tok_half, cot_half = (
        lax.dynamic_slice_in_dim(a, s * half, half, 1) for a in (tokens, cotangent)
    )
    held = {"tok_a": tok_half, "cot_a": cot_half, "mark": jnp.zeros((8, 128), F32)}
    for i, p in enumerate(parts):
        held["own%d" % i] = held["up%d0" % i] = held["down%d0" % i] = p
    order = [(i, step) for step in range(1, places) for i in range(len(parts))]
    sent = []
    for n, (i, step) in enumerate(order):
        if n == 1:
            held["tok_a"] = lax.ppermute(held["tok_a"], "grp", SWAP)
            held["cot_a"] = lax.ppermute(held["cot_a"], "grp", SWAP)
        if n >= 2:
            names = sent[n - 2]
            names += ("tok_a",) if n - 2 == TOK_TIE else ()
            names += ("cot_a",) if n - 2 == FAR_TIE else ()
            marker(held, FLOPS, *names)
        sent.append(hop(held, i, step, places))
    tok_a, cot_a = held["tok_a"], held["cot_a"]
    tok_b, cot_b = (lax.ppermute(a, "sub", SWAP) for a in (tok_a, cot_a))
    early, late = [
        [held["own%d" % i]]
        + [held["%s%d%d" % (way, i, step)] for way in ("up", "down") for step in range(1, places)]
        for i in range(len(parts))
    ]

    sums_shape = pltpu.VMEM((both, model_width), F32)
    piece = pltpu.VMEM((2, both, model_width // 4), BF16)
    tok_rows, sums = both_rows(meta, tokens, tok_a, tok_b)
    cot_rows, sums_g = both_rows(meta, cotangent, cot_a, cot_b)
    row_arrays = [tok_rows, cot_rows]
    scalars = [meta, in_blocks, out_blocks]
    size = w_in.shape[3]
    blocks_shape = w_in.shape[1:2] + (size, size)
    sums, sums_g = call(
        early_kernel,
        "early",
        0,
        scalars,
        early,
        row_arrays + [sums, sums_g],
        [sums_shape] * 2,
        {2: 0, 3: 1},
        [pltpu.VMEM((2 * counts[0],) + blocks_shape, BF16)],
    )
    w_shape = pltpu.VMEM((2 * counts[1],) + blocks_shape, BF16)
    slopes_shape = pltpu.VMEM((counts[1], both, size), F32)
    keep, send, late_w, slopes, _, sums_g = call(
        late_out_kernel,
        "late_out",
        firsts[1],
        scalars,
        late,
        [row_arrays[0], held["mark"], sums, sums_g],
        [piece, piece, w_shape, slopes_shape, sums_shape, sums_shape],
        {2: 4, 3: 5},
    )
    (backs,) = in_vmem(
        late_back_kernel,
        "late_back",
        firsts[1],
        [meta, out_blocks],
        [row_arrays[1], late_w, slopes],
        [pltpu.VMEM((counts[1], both, size), BF16)],
        {},
        BACK_FLOPS,
    )
    keep_g, send_g, _ = in_vmem(
        late_grad_kernel,
        "late_grad",
        firsts[1],
        [meta, in_blocks],
        [late_w, backs, sums_g],
        [piece, piece, sums_shape],
        {2: 2},
        GRAD_FLOPS,
    )
    return reduce_pair(keep, send), reduce_pair(keep_g, send_g)


BACK_FLOPS = 10**9
GRAD_FLOPS = 10**9


def solution(mesh):
    in_specs = (
        P(("grp", "seq"), None),
        P(("grp", "seq"), None),
        P(("mdl", "sub"), None, "seq", None),
        P(("mdl", "sub"), None, "seq", None),
        P(("mdl", "sub"), None),
        P(("mdl", "sub"), None),
    )
    out_specs = (P(("grp", "seq"), ("mdl", "sub")), P(("grp", "seq"), ("mdl", "sub")))
    sizes = tuple(mesh.shape[a] for a in ("grp", "seq", "mdl", "sub"))
    local = fast if sizes == (2, 4, 2, 2) else general
    return jax.shard_map(local, mesh=mesh, in_specs=in_specs, out_specs=out_specs, check_vma=False)
```
